32 devices in a mesh: bz: 4 (over z), bxy: 8 (over y, x, core).
Axes of the slice: x: 2, y: 2, z: 4, core: 2. Of those that a mesh axis runs over, the one named last changes fastest.
Arguments:
- pdfs: float32 [19, 4, 256, 4096], P(None, None, 'bxy', 'bz'), may hold values from 0.008 to 0.57, as said below
- relax: float32 [4, 256, 4096], P(None, 'bxy', 'bz'), may hold values from 0.6 to 1.9
- fluid: int32 [4, 256, 4096], P(None, 'bxy', 'bz'), may hold values 0 or 1
- targets: int32 [4, 8, 4], P('bz', 'bxy'), may hold values from 0 to 31, as said below
Outputs:
- moved: float32 [19, 4, 256, 4096], P(None, None, 'bxy', 'bz')
The draws below stay inside these ranges and needn't reach their ends.
Inputs may be any that keep to these rules, and one draw needn't show every extreme that they name: `pdfs`: every entry is positive. Within each row along bz, targets is a permutation of the 32 positions; a block's new owner is its owner or the owner just before or after it along bxy (no wrap), and at most 2 blocks of one owner go to one neighbouring owner.
All inputs are finite; a program needn't handle non-finite values. No bound on the sum of `fluid` on one device may be relied on, other than what follows from the above.
Results may differ from the reference program's by a relative error of at most 0.0003.
Values sent between devices are 32-bit elements; how exact they have to be, the bound alone decides.
A program may use at most 192 MiB of HBM per device.

```python
import jax
import jax.numpy as jnp

EDGE = 32
BLK_DEV = 4
STEPS = 2
MOVE = 2
NX = 256
NYZ = 4096
N_BZ = 4
N_BXY = 8


WEIGHT_TABLE = (1.0 / 3.0,) + (1.0 / 18.0,) * 6 + (1.0 / 36.0,) * 12


def draw_pdfs(key, part):
    shape = (19, BLK_DEV, NX, NYZ)
    weights = jnp.array(WEIGHT_TABLE, jnp.float32).reshape((19, 1, 1, 1))
    factor = 1.0 + 0.35 * jnp.clip(jax.random.normal(key, shape, jnp.float32), -2.0, 2.0)
    return (weights * factor).astype(jnp.float32)


def draw_targets(key, part):
    rows = N_BZ
    owners = N_BXY
    blocks = BLK_DEV
    keys = jax.random.split(key, 3)
    bounds = jax.random.randint(keys[0], (rows, owners - 1), 1, MOVE + 1).astype(jnp.int32)
    forced = jax.random.randint(keys[1], (rows, 1), 0, owners - 1).astype(jnp.int32)
    bound_ids = jnp.arange(owners - 1, dtype=jnp.int32)[None, :]
    bounds = jnp.where(bound_ids == forced, MOVE, bounds)
    zeros = jnp.zeros((rows, 1), jnp.int32)
    right_count = jnp.concatenate([bounds, zeros], axis=1)
    left_count = jnp.concatenate([zeros, bounds], axis=1)
    scores = jax.random.randint(keys[2], (rows, owners, blocks), 0, 1 << 16).astype(jnp.int32) * blocks
    scores = scores + jnp.arange(blocks, dtype=jnp.int32)[None, None, :]
    order = jnp.argsort(scores, axis=-1).astype(jnp.int32)
    rank = jnp.argsort(order, axis=-1).astype(jnp.int32)
    order_next = jnp.roll(order, -1, axis=1)
    right_next = jnp.roll(right_count, -1, axis=1)
    order_prev = jnp.roll(order, 1, axis=1)
    right_here = right_count[:, :, None]
    left_here = left_count[:, :, None]
    right_index = jnp.clip(right_next[:, :, None] + rank, 0, blocks - 1)
    left_index = jnp.clip(rank - right_here, 0, blocks - 1)
    right_slot = jnp.take_along_axis(order_next, right_index, axis=-1)
    left_slot = jnp.take_along_axis(order_prev, left_index, axis=-1)
    owner_ids = jnp.arange(owners, dtype=jnp.int32)[None, :, None]
    slots = jnp.arange(blocks, dtype=jnp.int32)[None, None, :]
    goes_right = rank < right_here
    goes_left = (rank >= right_here) & (rank < right_here + left_here)
    result = jnp.where(goes_right, (owner_ids + 1) * blocks + right_slot, jnp.where(goes_left, (owner_ids - 1) * blocks + left_slot, owner_ids * blocks + slots))
    return result.astype(jnp.int32)


def touch_ends(drawn, stream_key, low, high):
    index_at = [jax.random.randint(jax.random.fold_in(stream_key, axis), (), 0, length) for axis, length in enumerate(drawn.shape)]
    widest = drawn.shape.index(max(drawn.shape))
    beside = index_at[:widest] + [(index_at[widest] + 1) % drawn.shape[widest]] + index_at[widest + 1:]
    return drawn.at[tuple(index_at)].set(low).at[tuple(beside)].set(high)


def levels(rng, extent, cuts, low, top_value):
    level = 1.0
    for axis_at, blocks in cuts:
        draws = jax.random.uniform(jax.random.fold_in(jax.random.fold_in(rng, 6), axis_at), (blocks,), jnp.float32, low / len(cuts), top_value / len(cuts))
        level = level * jnp.repeat(jnp.exp(draws), extent[axis_at] // blocks).reshape((-1,) + (1,) * (len(extent) - 1 - axis_at))
    return level


def setup_inputs(seed: int = 0) -> dict:
    arg_keys = jax.random.split(jax.random.key(seed), 5)
    return {
        "pdfs": draw_pdfs(jax.random.fold_in(arg_keys[4], 71), 0),
        "relax": jnp.clip(0.6 + 1.3 * jax.random.uniform(arg_keys[1], (BLK_DEV, NX, NYZ), jnp.float32) ** levels(arg_keys[1], (BLK_DEV, NX, NYZ), ((1, 8), (2, 4)), -0.2, 0.2), 0.6, 1.9),
        "fluid": touch_ends((jax.random.randint(arg_keys[2], (BLK_DEV, NX, NYZ), 0, 5) < 4).astype(jnp.int32), jax.random.fold_in(arg_keys[2], 1), 0, 1),
        "targets": draw_targets(jax.random.fold_in(arg_keys[4], 71), 0),
    }


VELOCITIES = ((0, 0, 0), (1, 0, 0), (-1, 0, 0), (0, 1, 0), (0, -1, 0), (0, 0, 1), (0, 0, -1),
              (1, 1, 0), (-1, -1, 0), (1, -1, 0), (-1, 1, 0), (1, 0, 1), (-1, 0, -1),
              (1, 0, -1), (-1, 0, 1), (0, 1, 1), (0, -1, -1), (0, 1, -1), (0, -1, 1))
OPPOSITE = (0, 2, 1, 4, 3, 6, 5, 8, 7, 10, 9, 12, 11, 14, 13, 16, 15, 18, 17)
WEIGHTS = (1.0 / 3.0,) + (1.0 / 18.0,) * 6 + (1.0 / 36.0,) * 12


def component(populations, axis_number):
    total = jnp.zeros_like(populations[0])
    for index, velocity in enumerate(VELOCITIES):
        if velocity[axis_number] == 1:
            total = total + populations[index]
        elif velocity[axis_number] == -1:
            total = total - populations[index]
    return total


def collide(populations, rates):
    density = jnp.zeros_like(populations[0])
    for index in range(19):
        density = density + populations[index]
    speed = [component(populations, axis_number) / density for axis_number in range(3)]
    square = speed[0] * speed[0] + speed[1] * speed[1] + speed[2] * speed[2]
    result = []
    for index, velocity in enumerate(VELOCITIES):
        along = jnp.zeros_like(density)
        for axis_number in range(3):
            if velocity[axis_number] == 1:
                along = along + speed[axis_number]
            elif velocity[axis_number] == -1:
                along = along - speed[axis_number]
        balance = WEIGHTS[index] * density * (1.0 + 3.0 * along + 4.5 * along * along - 1.5 * square)
        result.append(populations[index] + rates * (balance - populations[index]))
    return jnp.stack(result)


def pulled(field, velocity):
    padded = jnp.pad(field, 1)
    sizes = field.shape
    return padded[1 - velocity[0]:1 - velocity[0] + sizes[0],
                  1 - velocity[1]:1 - velocity[1] + sizes[1],
                  1 - velocity[2]:1 - velocity[2] + sizes[2]]


def to_grid(array):
    lead = array.shape[:-3]
    blocks, width_x, width_yz = array.shape[-3:]
    shaped = array.reshape(lead + (blocks, width_x, width_yz // EDGE, EDGE))
    shaped = jnp.moveaxis(shaped, -4, -2)
    return shaped.reshape(lead + (width_x, width_yz // EDGE, blocks * EDGE))


def from_grid(grid):
    width_x, width_y, width_z = grid.shape[1:]
    blocks = width_z // EDGE
    shaped = grid.reshape((19, width_x, width_y, blocks, EDGE))
    shaped = jnp.moveaxis(shaped, -2, -4)
    return shaped.reshape((19, blocks, width_x, width_y * EDGE))


def reference(pdfs, relax, fluid, targets):
    blocks = pdfs.shape[1]
    fluid_grid = to_grid(fluid)
    fluid_cells = fluid_grid > 0
    fluid_value = fluid_grid.astype(jnp.float32)
    rates = to_grid(relax)
    populations = to_grid(pdfs)
    for step in range(STEPS):
        post = collide(populations, rates)
        result = []
        for index, velocity in enumerate(VELOCITIES):
            source = pulled(fluid_value, velocity)
            incoming = pulled(post[index], velocity)
            value = jnp.where(source > 0.5, incoming, post[OPPOSITE[index]])
            result.append(jnp.where(fluid_cells, value, populations[index]))
        populations = jnp.stack(result)
    final = from_grid(populations)
    count = N_BXY * blocks
    grouped = final.reshape((19, blocks, N_BXY, EDGE, N_BZ, EDGE * EDGE))
    grouped = jnp.transpose(grouped, (4, 2, 1, 0, 3, 5)).reshape((N_BZ, count, 19, EDGE, EDGE * EDGE))
    flat = targets.reshape((N_BZ, count)).astype(jnp.int32)
    row_index = jnp.broadcast_to(jnp.arange(N_BZ, dtype=jnp.int32)[:, None], (N_BZ, count))
    anchor = jnp.zeros((N_BZ, count), jnp.int32).at[row_index, flat].set(
        jnp.broadcast_to(jnp.arange(count, dtype=jnp.int32)[None, :], (N_BZ, count)))
    placed = jnp.take_along_axis(grouped, anchor[:, :, None, None, None], axis=1)
    placed = placed.reshape((N_BZ, N_BXY, blocks, 19, EDGE, EDGE * EDGE))
    placed = jnp.transpose(placed, (3, 2, 1, 4, 0, 5))
    return placed.reshape((19, blocks, N_BXY * EDGE, N_BZ * EDGE * EDGE))
```

```python
import functools

import jax
import jax.numpy as jnp
from jax import lax
from jax.experimental import pallas as pl
from jax.experimental.pallas import tpu as pltpu
from jax.sharding import PartitionSpec as P

MESH = pl.DeviceIdType.MESH
VELOCITIES = (
    (0, 0, 0), (1, 0, 0), (-1, 0, 0), (0, 1, 0), (0, -1, 0), (0, 0, 1), (0, 0, -1),
    (1, 1, 0), (-1, -1, 0), (1, -1, 0), (-1, 1, 0), (1, 0, 1), (-1, 0, -1),
    (1, 0, -1), (-1, 0, 1), (0, 1, 1), (0, -1, -1), (0, 1, -1), (0, -1, 1),
)
OPPOSITE = (0, 2, 1, 4, 3, 6, 5, 8, 7, 10, 9, 12, 11, 14, 13, 16, 15, 18, 17)
Q = 19
ORDER = (5, 11, 14, 15, 18, 6, 12, 13, 16, 17, 0, 1, 2, 3, 4, 7, 8, 9, 10)
AT = tuple(ORDER.index(i) for i in range(Q))
NATURAL = tuple(range(Q))
Y_SENT = tuple(tuple(i for i in range(Q) if VELOCITIES[i][1] == c) for c in (1, -1))
X_SENT = tuple(tuple(i for i in range(Q) if VELOCITIES[i][0] == c) for c in (1, -1))
CORNERS = (7, 8, 9, 10)
SIDE = {1: 0, -1: 1}
VMEM_LIMIT = 60 * 1024 * 1024


def collide(f, rate):
    pair = {i: (f[i] + f[i + 1], f[i] - f[i + 1]) for i in range(1, Q, 2)}
    density = f[0]
    for i in range(1, Q, 2):
        density = density + pair[i][0]
    scale = 3.0 / density
    flow = []
    for axis in range(3):
        total = None
        for i in range(1, Q, 2):
            c = VELOCITIES[i][axis]
            if c:
                d = pair[i][1]
                total = d if total is None else (total + d if c == 1 else total - d)
        flow.append(total * scale)
    base = 1.0 - (flow[0] * flow[0] + flow[1] * flow[1] + flow[2] * flow[2]) * (1.0 / 6.0)
    keep = 1.0 - rate
    drive = rate * density
    post = [None] * Q
    post[0] = keep * f[0] + (drive * (1.0 / 3.0)) * base
    near, far = drive * (1.0 / 18.0), drive * (1.0 / 36.0)
    for i in range(1, Q, 2):
        along = None
        for axis in range(3):
            c = VELOCITIES[i][axis]
            if c:
                along = flow[axis] if along is None else (along + flow[axis] if c == 1 else along - flow[axis])
        even = base + 0.5 * (along * along)
        weight = near if i < 7 else far
        post[i] = keep * f[i] + weight * (even + along)
        post[i + 1] = keep * f[i + 1] + weight * (even - along)
    return post


def collide_block(read, relax_ref, fluid_ref, post_ref):
    rows, width = relax_ref.shape[1:]
    tiles = width // 128

    def body(step, carry):
        r = pl.multiple_of((step // tiles) * 8, 8)
        c = pl.multiple_of((step % tiles) * 128, 128)
        at = (pl.ds(r, 8), pl.ds(c, 128))
        rate = jnp.where(fluid_ref[(0,) + at] > 0, relax_ref[(0,) + at], 0.0)
        post = collide([read(i, at) for i in range(Q)], rate)
        for i in range(Q):
            post_ref[(AT[i], 0) + at] = post[i]
        return carry

    lax.fori_loop(0, (rows // 8) * tiles, body, 0)


def emit_halo(slot, last, edge, post_ref, fluid_ref, ys_ref, xs_ref, cs_ref):
    rows, width = fluid_ref.shape[1:]
    lane = lax.broadcasted_iota(jnp.int32, (rows, 128), 1)
    mine = lane // edge == slot
    for side, first in ((0, width - 128), (1, 0)):
        turn = slot * edge + (edge if side == 0 else 0)
        turn = lax.rem(turn, 128)
        for n in range(6):
            if n < 5:
                tile = post_ref[AT[Y_SENT[side][n]], 0, :, first:first + 128]
            else:
                tile = fluid_ref[0, :, first:first + 128].astype(jnp.float32)
            ys_ref[side, n] = jnp.where(mine, pltpu.roll(tile, turn, 1), ys_ref[side, n])
    for side, row in ((0, rows - 1), (1, 0)):
        for n in range(5):
            xs_ref[side, 0, n:n + 1, :] = post_ref[AT[X_SENT[side][n]], 0, row:row + 1, :]
        xs_ref[side, 0, 5:6, :] = fluid_ref[0, row:row + 1, :].astype(jnp.float32)
        xs_ref[side, 0, 6:8, :] = jnp.zeros((2, width), jnp.float32)

    @pl.when(last)
    def _():
        for k, i in enumerate(CORNERS):
            cx, cy, _z = VELOCITIES[i]
            row = rows - 1 if cx == 1 else 0
            ys = SIDE[cy]
            cs_ref[k, 0:1, :] = ys_ref[ys, Y_SENT[ys].index(i), row:row + 1, :]
            cs_ref[k, 1:2, :] = ys_ref[ys, 5, row:row + 1, :]
            cs_ref[k, 2:8, :] = jnp.zeros((6, 128), jnp.float32)


def first_kernel(edge, pdfs_ref, relax_ref, fluid_ref, post_ref, ys_ref, xs_ref, cs_ref):
    slot = pl.program_id(0)
    collide_block(lambda i, at: pdfs_ref[(i, 0) + at], relax_ref, fluid_ref, post_ref)
    emit_halo(slot, slot == pl.num_programs(0) - 1, edge, post_ref, fluid_ref, ys_ref, xs_ref, cs_ref)


def halo_kernel(ys, xs, cs, yr, xr, cr, send_sem, recv_sem):
    nz, nb = lax.axis_size("bz"), lax.axis_size("bxy")
    z, b = lax.axis_index("bz"), lax.axis_index("bxy")

    def device(dz, db):
        return (lax.rem(z + dz + nz, nz), lax.rem(b + db + nb, nb))

    routes = [(ys.at[0], yr.at[0], 1, 0), (ys.at[1], yr.at[1], -1, 0),
              (xs.at[0], xr.at[0], 0, 1), (xs.at[1], xr.at[1], 0, -1)]
    for k, i in enumerate(CORNERS):
        routes.append((cs.at[k], cr.at[k], VELOCITIES[i][1], VELOCITIES[i][0]))
    barrier = pltpu.get_barrier_semaphore()
    for _s, _d, dz, db in routes:
        pl.semaphore_signal(barrier, inc=1, device_id=device(dz, db), device_id_type=MESH)
    pl.semaphore_wait(barrier, len(routes))
    copies = []
    for n, (src, dst, dz, db) in enumerate(routes):
        copy = pltpu.make_async_remote_copy(
            src_ref=src, dst_ref=dst, send_sem=send_sem.at[n], recv_sem=recv_sem.at[n],
            device_id=device(dz, db), device_id_type=MESH)
        copy.start()
        copies.append(copy)
    for copy in copies:
        copy.wait()


def exchange(ys, xs, cs):
    vmem = pl.BlockSpec(memory_space=pltpu.VMEM)
    return pl.pallas_call(
        halo_kernel,
        out_shape=[jax.ShapeDtypeStruct(a.shape, a.dtype) for a in (ys, xs, cs)],
        in_specs=[vmem] * 3,
        out_specs=[vmem] * 3,
        scratch_shapes=[pltpu.SemaphoreType.DMA((8,)), pltpu.SemaphoreType.DMA((8,))],
        compiler_params=pltpu.CompilerParams(collective_id=0, has_side_effects=True,
                                             vmem_limit_bytes=8 * 1024 * 1024),
        name="halo",
    )(ys, xs, cs)


def lane_shift(velocity, slot, edge, here, below, above, beside):
    _cx, cy, cz = velocity
    width = here.shape[1]
    step = cy * edge + cz
    moved = here if step == 0 else pltpu.roll(here, step % width, 1)
    if cz:
        depth = lax.broadcasted_iota(jnp.int32, here.shape, 1) % edge
        other, face = (below, 0) if cz == 1 else (above, edge - 1)
        carry = step - cz * edge
        wrapped = other if carry == 0 else pltpu.roll(other, carry % width, 1)
        moved = jnp.where(depth == face, wrapped, moved)
    if cy:
        lane = lax.broadcasted_iota(jnp.int32, (here.shape[0], 128), 1)
        offset = 128 if cy == 1 else 256 - edge
        outside = pltpu.roll(beside, lax.rem(offset + cz + 128 - slot * edge, 128), 1)
        if cy == 1:
            moved = jnp.concatenate([jnp.where(lane < edge, outside, moved[:, :128]), moved[:, 128:]], axis=1)
        else:
            moved = jnp.concatenate(
                [moved[:, :-128], jnp.where(lane >= 128 - edge, outside, moved[:, -128:])], axis=1)
    return moved


def arrive(i, slot, edge, slots, here, below, above, yr_ref, xr_ref, cr_ref, fluid):
    velocity = cx, cy, cz = VELOCITIES[i]
    beside = None
    if cy:
        side = SIDE[cy]
        beside = yr_ref[side, 5 if fluid else Y_SENT[side].index(i)]
    moved = lane_shift(velocity, slot, edge, here, below, above, beside)
    if cx:
        side = SIDE[cx]
        row = 5 if fluid else X_SENT[side].index(i)
        rows = moved.shape[0]

        def plane(s):
            return jnp.broadcast_to(xr_ref[side, s, row:row + 1, :], (8, moved.shape[1]))

        corner = None
        if cy:
            k = CORNERS.index(i)
            n = 1 if fluid else 0
            corner = jnp.broadcast_to(cr_ref[k, n:n + 1, :], (8, 128))
        entering = lane_shift(
            velocity, slot, edge, plane(slot), plane(jnp.maximum(slot - 1, 0)) if cz == 1 else None,
            plane(jnp.minimum(slot + 1, slots - 1)) if cz == -1 else None, corner)
        index = lax.broadcasted_iota(jnp.int32, (8, moved.shape[1]), 0)
        moved = pltpu.roll(moved, cx % rows, 0)
        if cx == 1:
            moved = jnp.concatenate([jnp.where(index == 0, entering, moved[:8]), moved[8:]], axis=0)
        else:
            moved = jnp.concatenate([moved[:-8], jnp.where(index == 7, entering, moved[-8:])], axis=0)
    return moved


def stream_block(slot, edge, slots, mask_ref, post_ref, below_ref, above_ref, yr_ref, xr_ref, cr_ref, write):
    for i in range(Q):
        cz = VELOCITIES[i][2]
        own = post_ref[AT[i], 0]
        if i == 0:
            write(0, own)
            continue
        value = arrive(
            i, slot, edge, slots, own, below_ref[AT[i], 0] if cz == 1 else None,
            above_ref[AT[i] - 5, 0] if cz == -1 else None, yr_ref, xr_ref, cr_ref, False)
        mask = mask_ref[0]
        stay = jnp.where(mask > 0, post_ref[AT[OPPOSITE[i]], 0], own)
        write(i, jnp.where((mask & (1 << i)) != 0, value, stay))


def middle_kernel(edge, ends_ref, post_ref, below_ref, above_ref, relax_ref, fluid_ref, fbelow_ref, fabove_ref,
                  yr_ref, xr_ref, cr_ref, out_ref, mask_ref, ys_ref, xs_ref, cs_ref, next_ref):
    slot, slots = pl.program_id(0), pl.num_programs(0)
    rows, width = fluid_ref.shape[1:]
    row = lax.broadcasted_iota(jnp.int32, (rows, width), 0)
    lane = lax.broadcasted_iota(jnp.int32, (rows, width), 1)
    depth = lane % edge
    fluid = fluid_ref[0].astype(jnp.float32)
    bits = jnp.ones((rows, width), jnp.int32)
    for i in range(1, Q):
        cx, cy, cz = VELOCITIES[i]
        source = arrive(i, slot, edge, slots, fluid, fbelow_ref[0].astype(jnp.float32) if cz == 1 else None,
                        fabove_ref[0].astype(jnp.float32) if cz == -1 else None, yr_ref, xr_ref, cr_ref, True)
        bit = jnp.where(source > 0.5, 1 << i, 0)
        if cx:
            edge_row = 0 if cx == 1 else rows - 1
            bit = jnp.where((row == edge_row) & (ends_ref[0 if cx == 1 else 1] > 0), 0, bit)
        if cy:
            outer = lane < edge if cy == 1 else lane >= width - edge
            bit = jnp.where(outer & (ends_ref[2 if cy == 1 else 3] > 0), 0, bit)
        if cz:
            final = 0 if cz == 1 else slots - 1
            face = 0 if cz == 1 else edge - 1
            bit = jnp.where((depth == face) & (slot == final), 0, bit)
        bits = bits | bit
    mask_ref[0] = jnp.where(fluid_ref[0] > 0, bits, 0)

    def write(i, value):
        next_ref[i] = value

    stream_block(slot, edge, slots, mask_ref, post_ref, below_ref, above_ref, yr_ref, xr_ref, cr_ref, write)
    collide_block(lambda i, at: next_ref[(i,) + at], relax_ref, fluid_ref, out_ref)
    emit_halo(slot, slot == slots - 1, edge, out_ref, fluid_ref, ys_ref, xs_ref, cs_ref)


def last_kernel(edge, mask_ref, post_ref, below_ref, above_ref, yr_ref, xr_ref, cr_ref, out_ref):
    def write(i, value):
        out_ref[i, 0] = value

    stream_block(pl.program_id(0), edge, pl.num_programs(0), mask_ref, post_ref, below_ref, above_ref,
                 yr_ref, xr_ref, cr_ref, write)


def pack_kernel(pick_ref, source_ref, out_ref):
    out_ref[...] = source_ref[...]


def pack(final, pick):
    q, _blocks, rows, width = final.shape
    count = pick.shape[0]
    parts = 2 if rows % 16 == 0 else 1
    block = (q, 1, rows // parts, width)
    return pl.pallas_call(
        pack_kernel,
        out_shape=jax.ShapeDtypeStruct((q, count, rows, width), final.dtype),
        grid_spec=pltpu.PrefetchScalarGridSpec(
            num_scalar_prefetch=1, grid=(count, parts),
            in_specs=[pl.BlockSpec(block, lambda g, h, pick: (0, pick[g], h, 0))],
            out_specs=pl.BlockSpec(block, lambda g, h, pick: (0, g, h, 0))),
        compiler_params=pltpu.CompilerParams(vmem_limit_bytes=VMEM_LIMIT),
        name="pack",
    )(pick, final)


def place_kernel(table_ref, final_ref, left_ref, right_ref, out_ref):
    kind = table_ref[pl.program_id(0), 0]

    @pl.when(kind == 0)
    def _():
        out_ref[...] = final_ref[...]

    @pl.when(kind == 1)
    def _():
        out_ref[...] = left_ref[...]

    @pl.when(kind == 2)
    def _():
        out_ref[...] = right_ref[...]


def place(final, left, right, table):
    q, blocks, rows, width = final.shape
    parts = 2 if rows % 16 == 0 else 1
    block = (q, 1, rows // parts, width)

    def taken(kind):
        def index(k, h, table):
            used = table[k, 0] == kind
            return (0, jnp.where(used, table[k, 1], 0), jnp.where(used, h, 0), 0)
        return pl.BlockSpec(block, index)

    return pl.pallas_call(
        place_kernel,
        out_shape=jax.ShapeDtypeStruct(final.shape, final.dtype),
        grid_spec=pltpu.PrefetchScalarGridSpec(
            num_scalar_prefetch=1, grid=(blocks, parts),
            in_specs=[taken(0), taken(1), taken(2)],
            out_specs=pl.BlockSpec(block, lambda k, h, table: (0, k, h, 0))),
        compiler_params=pltpu.CompilerParams(vmem_limit_bytes=VMEM_LIMIT),
        name="place",
    )(table, final, left, right)


def from_behind(value, axis, steps):
    count = lax.axis_size(axis)
    leading, last = (max(0, -steps), min(count, count - steps))
    return lax.ppermute(value, axis, [(source, source + steps) for source in range(leading, last)])


def routes_of(targets, blocks):
    here = lax.axis_index("bxy")
    capacity = blocks // 2
    goal = targets.reshape((blocks,))
    left = from_behind(goal + 1, "bxy", 1) - 1
    right = from_behind(goal + 1, "bxy", -1) - 1
    numbers = jnp.arange(blocks, dtype=jnp.int32)
    ranks = jnp.arange(capacity, dtype=jnp.int32)

    def rank(going):
        return jnp.sum((going[None, :] & (numbers[None, :] < numbers[:, None])).astype(jnp.int32), axis=1)

    def picked(going):
        hit = going[:, None] & (rank(going)[:, None] == ranks[None, :])
        return jnp.sum(jnp.where(hit, numbers[:, None], 0), axis=0)

    def reaching(whose, from_index):
        going = (whose // blocks == here) & (whose >= 0)
        hit = going[:, None] & (whose[:, None] - here * blocks == numbers[None, :])
        return jnp.any(hit, axis=0), jnp.sum(jnp.where(hit, from_index(going)[:, None], 0), axis=0)

    _own, own_index = reaching(goal, lambda going: numbers)
    is_left, left_index = reaching(left, rank)
    is_right, right_index = reaching(right, rank)
    kind = jnp.where(is_left, 1, jnp.where(is_right, 2, 0))
    index = jnp.where(is_left, left_index, jnp.where(is_right, right_index, own_index))
    table = jnp.stack([kind, index], axis=1).astype(jnp.int32)
    return picked(goal // blocks == here + 1), picked(goal // blocks == here - 1), table


def on_device(pdfs, relax, fluid, targets):
    q, blocks, rows, width = pdfs.shape
    edge = rows
    f32 = jnp.float32
    go_right, go_left, table = routes_of(targets, blocks)
    here, row = lax.axis_index("bxy"), lax.axis_index("bz")
    ends = jnp.stack([here == 0, here == lax.axis_size("bxy") - 1, row == 0,
                      row == lax.axis_size("bz") - 1]).astype(jnp.int32)
    full = pl.BlockSpec((q, 1, rows, width), lambda s: (0, s, 0, 0))
    cell = pl.BlockSpec((1, rows, width), lambda s: (s, 0, 0))
    cell_below = pl.BlockSpec((1, rows, width), lambda s: (jnp.maximum(s - 1, 0), 0, 0))
    cell_above = pl.BlockSpec((1, rows, width), lambda s: (jnp.minimum(s + 1, blocks - 1), 0, 0))
    below = pl.BlockSpec((5, 1, rows, width), lambda s: (0, jnp.maximum(s - 1, 0), 0, 0))
    above = pl.BlockSpec((5, 1, rows, width), lambda s: (1, jnp.minimum(s + 1, blocks - 1), 0, 0))
    y_shape, x_shape, c_shape = (2, 6, rows, 128), (2, blocks, 8, width), (4, 8, 128)
    y_spec = pl.BlockSpec(y_shape, lambda s: (0, 0, 0, 0))
    x_all = pl.BlockSpec(x_shape, lambda s: (0, 0, 0, 0))
    x_spec = pl.BlockSpec((2, 1, 8, width), lambda s: (0, s, 0, 0))
    c_spec = pl.BlockSpec(c_shape, lambda s: (0, 0, 0))
    halo_out = [jax.ShapeDtypeStruct(s, f32) for s in (y_shape, x_shape, c_shape)]
    big = jax.ShapeDtypeStruct(pdfs.shape, f32)
    params = pltpu.CompilerParams(vmem_limit_bytes=VMEM_LIMIT)

    post, ys, xs, cs = pl.pallas_call(
        functools.partial(first_kernel, edge), grid=(blocks,),
        out_shape=[big] + halo_out, in_specs=[full, cell, cell],
        out_specs=[full, y_spec, x_spec, c_spec], compiler_params=params, name="first",
    )(pdfs, relax, fluid)
    halo = exchange(ys, xs, cs)
    post, mask, ys, xs, cs = pl.pallas_call(
        functools.partial(middle_kernel, edge), grid=(blocks,),
        out_shape=[big, jax.ShapeDtypeStruct(fluid.shape, jnp.int32)] + halo_out,
        in_specs=[pl.BlockSpec(memory_space=pltpu.SMEM), full, below, above, cell, cell, cell_below, cell_above,
                  y_spec, x_all, c_spec],
        out_specs=[full, cell, y_spec, x_spec, c_spec],
        scratch_shapes=[pltpu.VMEM((q, rows, width), f32)], compiler_params=params, name="middle",
    )(ends, post, post, post, relax, fluid, fluid, fluid, *halo)
    halo = exchange(ys, xs, cs)
    final = pl.pallas_call(
        functools.partial(last_kernel, edge), grid=(blocks,),
        out_shape=big, in_specs=[cell, full, below, above, y_spec, x_all, c_spec],
        out_specs=full, compiler_params=params, name="last",
    )(mask, post, post, post, *halo)
    got_left = from_behind(pack(final, go_right), "bxy", 1)
    got_right = from_behind(pack(final, go_left), "bxy", -1)
    return place(final, got_left, got_right, table)


def solution(mesh):
    placed = (
        P(None, None, "bxy", "bz"),
        P(None, "bxy", "bz"),
        P(None, "bxy", "bz"),
        P("bz", "bxy", None),
    )
    return jax.shard_map(
        on_device, mesh=mesh, in_specs=placed, out_specs=P(None, None, "bxy", "bz"), check_vma=False
    )
```

```python
import functools
import math

import jax
import jax.numpy as jnp
from jax import lax
from jax.experimental import pallas as pl
from jax.experimental.pallas import tpu as pltpu
from jax.sharding import PartitionSpec as P

MESH = pl.DeviceIdType.MESH
VELOCITIES = (
    (0, 0, 0), (1, 0, 0), (-1, 0, 0), (0, 1, 0), (0, -1, 0), (0, 0, 1), (0, 0, -1),
    (1, 1, 0), (-1, -1, 0), (1, -1, 0), (-1, 1, 0), (1, 0, 1), (-1, 0, -1),
    (1, 0, -1), (-1, 0, 1), (0, 1, 1), (0, -1, -1), (0, 1, -1), (0, -1, 1),
)
OPPOSITE = (0, 2, 1, 4, 3, 6, 5, 8, 7, 10, 9, 12, 11, 14, 13, 16, 15, 18, 17)
Q = 19
ORDER = (5, 11, 14, 15, 18, 6, 12, 13, 16, 17, 0, 1, 2, 3, 4, 7, 8, 9, 10)
AT = tuple(ORDER.index(i) for i in range(Q))
NATURAL = tuple(range(Q))
Y_SENT = tuple(tuple(i for i in range(Q) if VELOCITIES[i][1] == c) for c in (1, -1))
X_SENT = tuple(tuple(i for i in range(Q) if VELOCITIES[i][0] == c) for c in (1, -1))
CORNERS = (7, 8, 9, 10)
SIDE = {1: 0, -1: 1}
VMEM_LIMIT = 60 * 1024 * 1024


def collide(f, rate):
    pair = {i: (f[i] + f[i + 1], f[i] - f[i + 1]) for i in range(1, Q, 2)}
    density = f[0]
    for i in range(1, Q, 2):
        density = density + pair[i][0]
    scale = 3.0 / density
    flow = []
    for axis in range(3):
        total = None
        for i in range(1, Q, 2):
            c = VELOCITIES[i][axis]
            if c:
                d = pair[i][1]
                total = d if total is None else (total + d if c == 1 else total - d)
        flow.append(total * scale)
    base = 1.0 - (flow[0] * flow[0] + flow[1] * flow[1] + flow[2] * flow[2]) * (1.0 / 6.0)
    keep = 1.0 - rate
    drive = rate * density
    post = [None] * Q
    post[0] = keep * f[0] + (drive * (1.0 / 3.0)) * base
    near, far = drive * (1.0 / 18.0), drive * (1.0 / 36.0)
    for i in range(1, Q, 2):
        along = None
        for axis in range(3):
            c = VELOCITIES[i][axis]
            if c:
                along = flow[axis] if along is None else (along + flow[axis] if c == 1 else along - flow[axis])
        even = base + 0.5 * (along * along)
        weight = near if i < 7 else far
        post[i] = keep * f[i] + weight * (even + along)
        post[i + 1] = keep * f[i + 1] + weight * (even - along)
    return post


def collide_block(read, relax_ref, fluid_ref, post_ref):
    rows, width = relax_ref.shape[1:]
    tiles = width // 128

    def body(step, carry):
        r = pl.multiple_of((step // tiles) * 8, 8)
        c = pl.multiple_of((step % tiles) * 128, 128)
        at = (pl.ds(r, 8), pl.ds(c, 128))
        rate = jnp.where(fluid_ref[(0,) + at] > 0, relax_ref[(0,) + at], 0.0)
        post = collide([read(i, at) for i in range(Q)], rate)
        for i in range(Q):
            post_ref[(AT[i], 0) + at] = post[i]
        return carry

    lax.fori_loop(0, (rows // 8) * tiles, body, 0)


def emit_halo(slot, last, edge, post_ref, fluid_ref, ys_ref, xs_ref, cs_ref):
    rows, width = fluid_ref.shape[1:]
    lane = lax.broadcasted_iota(jnp.int32, (rows, 128), 1)
    mine = lane // edge == slot
    for side, first in ((0, width - 128), (1, 0)):
        turn = slot * edge + (edge if side == 0 else 0)
        turn = lax.rem(turn, 128)
        for n in range(6):
            if n < 5:
                tile = post_ref[AT[Y_SENT[side][n]], 0, :, first:first + 128]
            else:
                tile = fluid_ref[0, :, first:first + 128].astype(jnp.float32)
            ys_ref[side, n] = jnp.where(mine, pltpu.roll(tile, turn, 1), ys_ref[side, n])
    for side, row in ((0, rows - 1), (1, 0)):
        for n in range(5):
            xs_ref[side, 0, n:n + 1, :] = post_ref[AT[X_SENT[side][n]], 0, row:row + 1, :]
        xs_ref[side, 0, 5:6, :] = fluid_ref[0, row:row + 1, :].astype(jnp.float32)
        xs_ref[side, 0, 6:8, :] = jnp.zeros((2, width), jnp.float32)

    @pl.when(last)
    def _():
        for k, i in enumerate(CORNERS):
            cx, cy, _z = VELOCITIES[i]
            row = rows - 1 if cx == 1 else 0
            ys = SIDE[cy]
            cs_ref[k, 0:1, :] = ys_ref[ys, Y_SENT[ys].index(i), row:row + 1, :]
            cs_ref[k, 1:2, :] = ys_ref[ys, 5, row:row + 1, :]
            cs_ref[k, 2:8, :] = jnp.zeros((6, 128), jnp.float32)


def first_kernel(edge, pdfs_ref, relax_ref, fluid_ref, post_ref, ys_ref, xs_ref, cs_ref):
    slot = pl.program_id(0)
    collide_block(lambda i, at: pdfs_ref[(i, 0) + at], relax_ref, fluid_ref, post_ref)
    emit_halo(slot, slot == pl.num_programs(0) - 1, edge, post_ref, fluid_ref, ys_ref, xs_ref, cs_ref)


def remote(src, dst, send_sem, recv_sem, device):
    return pltpu.make_async_remote_copy(
        src_ref=src, dst_ref=dst, send_sem=send_sem, recv_sem=recv_sem, device_id=device, device_id_type=MESH)


def halo_kernel(ys, xs, cs, yr, xr, cr, send_sem, recv_sem):
    nz, nb = lax.axis_size("bz"), lax.axis_size("bxy")
    z, b = lax.axis_index("bz"), lax.axis_index("bxy")

    def there(dz, db):
        exists = None
        for at, step, count in ((z, dz, nz), (b, db, nb)):
            if step:
                inside = at < count - 1 if step == 1 else at > 0
                exists = inside if exists is None else exists & inside
        return exists

    routes = [(ys.at[0], yr.at[0], 1, 0), (ys.at[1], yr.at[1], -1, 0),
              (xs.at[0], xr.at[0], 0, 1), (xs.at[1], xr.at[1], 0, -1)]
    for k, i in enumerate(CORNERS):
        routes.append((cs.at[k], cr.at[k], VELOCITIES[i][1], VELOCITIES[i][0]))
    barrier = pltpu.get_barrier_semaphore()
    count = 0
    for _s, _d, dz, db in routes:
        count = count + there(dz, db).astype(jnp.int32)

        @pl.when(there(dz, db))
        def _():
            pl.semaphore_signal(barrier, inc=1, device_id=(z + dz, b + db), device_id_type=MESH)

    pl.semaphore_wait(barrier, count)
    for n, (src, dst, dz, db) in enumerate(routes):
        @pl.when(there(dz, db))
        def _():
            remote(src, dst, send_sem.at[n], recv_sem.at[n], (z + dz, b + db)).start()

    for n, (src, dst, dz, db) in enumerate(routes):
        @pl.when(there(dz, db))
        def _():
            remote(src, dst, send_sem.at[n], recv_sem.at[n], (z + dz, b + db)).wait_send()

        @pl.when(there(-dz, -db))
        def _():
            remote(src, dst, send_sem.at[n], recv_sem.at[n], (z - dz, b - db)).wait_recv()


def exchange(ys, xs, cs):
    vmem = pl.BlockSpec(memory_space=pltpu.VMEM)
    return pl.pallas_call(
        halo_kernel,
        out_shape=[jax.ShapeDtypeStruct(a.shape, a.dtype) for a in (ys, xs, cs)],
        in_specs=[vmem] * 3,
        out_specs=[vmem] * 3,
        scratch_shapes=[pltpu.SemaphoreType.DMA((8,)), pltpu.SemaphoreType.DMA((8,))],
        compiler_params=pltpu.CompilerParams(collective_id=0, has_side_effects=True,
                                             vmem_limit_bytes=8 * 1024 * 1024),
        name="halo",
    )(ys, xs, cs)


def lane_shift(velocity, slot, edge, here, below, above, beside):
    _cx, cy, cz = velocity
    width = here.shape[1]
    step = cy * edge + cz
    moved = here if step == 0 else pltpu.roll(here, step % width, 1)
    if cz:
        depth = lax.broadcasted_iota(jnp.int32, here.shape, 1) % edge
        other, face = (below, 0) if cz == 1 else (above, edge - 1)
        carry = step - cz * edge
        wrapped = other if carry == 0 else pltpu.roll(other, carry % width, 1)
        moved = jnp.where(depth == face, wrapped, moved)
    if cy:
        lane = lax.broadcasted_iota(jnp.int32, (here.shape[0], 128), 1)
        offset = 128 if cy == 1 else 256 - edge
        outside = pltpu.roll(beside, lax.rem(offset + cz + 128 - slot * edge, 128), 1)
        if cy == 1:
            moved = jnp.concatenate([jnp.where(lane < edge, outside, moved[:, :128]), moved[:, 128:]], axis=1)
        else:
            moved = jnp.concatenate(
                [moved[:, :-128], jnp.where(lane >= 128 - edge, outside, moved[:, -128:])], axis=1)
    return moved


def arrive(i, slot, edge, slots, here, below, above, yr_ref, xr_ref, cr_ref, fluid):
    velocity = cx, cy, cz = VELOCITIES[i]
    beside = None
    if cy:
        side = SIDE[cy]
        beside = yr_ref[side, 5 if fluid else Y_SENT[side].index(i)]
    moved = lane_shift(velocity, slot, edge, here, below, above, beside)
    if cx:
        side = SIDE[cx]
        row = 5 if fluid else X_SENT[side].index(i)
        rows = moved.shape[0]

        def plane(s):
            return jnp.broadcast_to(xr_ref[side, s, row:row + 1, :], (8, moved.shape[1]))

        corner = None
        if cy:
            k = CORNERS.index(i)
            n = 1 if fluid else 0
            corner = jnp.broadcast_to(cr_ref[k, n:n + 1, :], (8, 128))
        entering = lane_shift(
            velocity, slot, edge, plane(slot), plane(jnp.maximum(slot - 1, 0)) if cz == 1 else None,
            plane(jnp.minimum(slot + 1, slots - 1)) if cz == -1 else None, corner)
        index = lax.broadcasted_iota(jnp.int32, (8, moved.shape[1]), 0)
        moved = pltpu.roll(moved, cx % rows, 0)
        if cx == 1:
            moved = jnp.concatenate([jnp.where(index == 0, entering, moved[:8]), moved[8:]], axis=0)
        else:
            moved = jnp.concatenate([moved[:-8], jnp.where(index == 7, entering, moved[-8:])], axis=0)
    return moved


def stream_block(slot, edge, slots, mask_ref, post_ref, below_ref, above_ref, yr_ref, xr_ref, cr_ref, write):
    for i in range(Q):
        cz = VELOCITIES[i][2]
        own = post_ref[AT[i], 0]
        if i == 0:
            write(0, own)
            continue
        value = arrive(
            i, slot, edge, slots, own, below_ref[AT[i], 0] if cz == 1 else None,
            above_ref[AT[i] - 5, 0] if cz == -1 else None, yr_ref, xr_ref, cr_ref, False)
        mask = mask_ref[0]
        stay = jnp.where(mask > 0, post_ref[AT[OPPOSITE[i]], 0], own)
        write(i, jnp.where((mask & (1 << i)) != 0, value, stay))


def middle_kernel(edge, ends_ref, post_ref, below_ref, above_ref, relax_ref, fluid_ref, fbelow_ref, fabove_ref,
                  yr_ref, xr_ref, cr_ref, out_ref, mask_ref, ys_ref, xs_ref, cs_ref, next_ref):
    slot, slots = pl.program_id(0), pl.num_programs(0)
    rows, width = fluid_ref.shape[1:]
    row = lax.broadcasted_iota(jnp.int32, (rows, width), 0)
    lane = lax.broadcasted_iota(jnp.int32, (rows, width), 1)
    depth = lane % edge
    fluid = fluid_ref[0].astype(jnp.float32)
    bits = jnp.ones((rows, width), jnp.int32)
    for i in range(1, Q):
        cx, cy, cz = VELOCITIES[i]
        source = arrive(i, slot, edge, slots, fluid, fbelow_ref[0].astype(jnp.float32) if cz == 1 else None,
                        fabove_ref[0].astype(jnp.float32) if cz == -1 else None, yr_ref, xr_ref, cr_ref, True)
        bit = jnp.where(source > 0.5, 1 << i, 0)
        if cx:
            edge_row = 0 if cx == 1 else rows - 1
            bit = jnp.where((row == edge_row) & (ends_ref[0 if cx == 1 else 1] > 0), 0, bit)
        if cy:
            outer = lane < edge if cy == 1 else lane >= width - edge
            bit = jnp.where(outer & (ends_ref[2 if cy == 1 else 3] > 0), 0, bit)
        if cz:
            final = 0 if cz == 1 else slots - 1
            face = 0 if cz == 1 else edge - 1
            bit = jnp.where((depth == face) & (slot == final), 0, bit)
        bits = bits | bit
    mask_ref[0] = jnp.where(fluid_ref[0] > 0, bits, 0)

    def write(i, value):
        next_ref[i] = value

    stream_block(slot, edge, slots, mask_ref, post_ref, below_ref, above_ref, yr_ref, xr_ref, cr_ref, write)
    collide_block(lambda i, at: next_ref[(i,) + at], relax_ref, fluid_ref, out_ref)
    emit_halo(slot, slot == slots - 1, edge, out_ref, fluid_ref, ys_ref, xs_ref, cs_ref)


def last_kernel(edge, plan_ref, mask_ref, post_ref, below_ref, above_ref, yr_ref, xr_ref, cr_ref,
                right_ref, left_ref, kept_ref, next_ref):
    def write(i, value):
        next_ref[i, 0] = value

    g = pl.program_id(0)
    stream_block(plan_ref[0, g], edge, pl.num_programs(0), mask_ref, post_ref, below_ref, above_ref,
                 yr_ref, xr_ref, cr_ref, write)
    for kind, out_ref in enumerate((right_ref, left_ref, kept_ref)):
        @pl.when(plan_ref[1, g] == kind)
        def _():
            def copy(i, carry):
                out_ref[i] = next_ref[i]
                return carry

            lax.fori_loop(0, Q, copy, 0)


def migrate_kernel(right, left, from_left, from_right, passing, send_sem, recv_sem):
    nb = lax.axis_size("bxy")
    z, b = lax.axis_index("bz"), lax.axis_index("bxy")
    half = (Q + 1) // 2
    cuts = (0, half // 2, half, half + (Q - half + 1) // 2, Q)
    chunks = [(n, slice(cuts[n], cuts[n + 1]), n < 2) for n in range(4)]
    across = math.isqrt(nb // 2)
    row = 2 * across
    bends = across == 2 and nb == 2 * row
    cut = row - 1 if bends else nb
    low, high = cut + 1 - row, cut + row
    no = b < 0
    goes_right, goes_left = (b < nb - 1) & (b != cut), (b > 0) & (b != cut + 1)
    at_cut, past_cut, is_low, is_high = (
        (b == cut, b == cut + 1, b == low, b == high) if bends else (no, no, no, no))
    meets = [(goes_right, b + 1), (goes_left, b - 1)]
    if bends:
        for who in (at_cut, past_cut):
            meets += [(who, low), (who, high)]
        for who in (is_low, is_high):
            meets += [(who, cut), (who, cut + 1)]
    barrier = pltpu.get_barrier_semaphore()
    count = 0
    for who, peer in meets:
        count = count + who.astype(jnp.int32)

        @pl.when(who)
        def _():
            pl.semaphore_signal(barrier, inc=1, device_id=(z, peer), device_id_type=MESH)

    pl.semaphore_wait(barrier, count)

    def copy(src, dst, c, part, sent, got, peer):
        return remote(src.at[part], dst.at[part], send_sem.at[sent, c], recv_sem.at[got, c], (z, peer))

    for c, part, first in chunks:
        @pl.when(goes_right)
        def _():
            copy(right, from_left, c, part, 0, 0, b + 1).start()

        @pl.when(goes_left)
        def _():
            copy(left, from_right, c, part, 1, 1, b - 1).start()

        if bends:
            @pl.when(at_cut)
            def _():
                copy(right, passing, c, part, 0, 2, low if first else high).start()

            @pl.when(past_cut)
            def _():
                copy(left, passing, c, part, 1, 2, high if first else low).start()

    if bends:
        for who, ahead in ((is_low, True), (is_high, False)):
            @pl.when(who)
            def _():
                for n in (0, 2, 1, 3):
                    c, part, first = chunks[n]
                    copy(right, passing, c, part, 2, 2, cut).wait_recv()
                    if first == ahead:
                        copy(passing, from_left, c, part, 2, 0, cut + 1).start()
                    else:
                        copy(passing, from_right, c, part, 2, 1, cut).start()
                for c, part, first in chunks:
                    copy(passing, from_left, c, part, 2, 0, cut).wait_send()

    for c, part, first in chunks:
        @pl.when(b < nb - 1)
        def _():
            copy(right, from_left, c, part, 0, 0, b + 1).wait_send()
            copy(left, from_right, c, part, 1, 1, b + 1).wait_recv()

        @pl.when(b > 0)
        def _():
            copy(left, from_right, c, part, 1, 1, b - 1).wait_send()
            copy(right, from_left, c, part, 0, 0, b - 1).wait_recv()


def migrate(right, left):
    hbm = pl.BlockSpec(memory_space=pl.ANY)
    shape = jax.ShapeDtypeStruct(right.shape, right.dtype)
    from_left, from_right, _passing = pl.pallas_call(
        migrate_kernel, out_shape=[shape] * 3, in_specs=[hbm] * 2, out_specs=[hbm] * 3,
        scratch_shapes=[pltpu.SemaphoreType.DMA((3, 4)), pltpu.SemaphoreType.DMA((3, 4))],
        compiler_params=pltpu.CompilerParams(collective_id=1, has_side_effects=True, vmem_limit_bytes=VMEM_LIMIT),
        name="migrate",
    )(right, left)
    return from_left, from_right


def place_kernel(table_ref, final_ref, left_ref, right_ref, out_ref):
    kind = table_ref[3, pl.program_id(0)]

    @pl.when(kind == 0)
    def _():
        out_ref[...] = final_ref[...]

    @pl.when(kind == 1)
    def _():
        out_ref[...] = left_ref[...]

    @pl.when(kind == 2)
    def _():
        out_ref[...] = right_ref[...]


def place(final, left, right, table):
    q, blocks, rows, width = final.shape
    block = (q, 1, rows, width)

    def taken(kind):
        return pl.BlockSpec(block, lambda k, table: (0, table[kind, k], 0, 0))

    return pl.pallas_call(
        place_kernel,
        out_shape=jax.ShapeDtypeStruct(final.shape, final.dtype),
        grid_spec=pltpu.PrefetchScalarGridSpec(
            num_scalar_prefetch=1, grid=(blocks,),
            in_specs=[taken(0), taken(1), taken(2)],
            out_specs=pl.BlockSpec(block, lambda k, table: (0, k, 0, 0))),
        compiler_params=pltpu.CompilerParams(vmem_limit_bytes=VMEM_LIMIT),
        name="place",
    )(table, final, left, right)


def from_behind(value, axis, steps):
    count = lax.axis_size(axis)
    leading, last = (max(0, -steps), min(count, count - steps))
    return lax.ppermute(value, axis, [(source, source + steps) for source in range(leading, last)])


def routes_of(targets, blocks):
    here = lax.axis_index("bxy")
    goal = targets.reshape((blocks,))
    left = from_behind(goal + 1, "bxy", 1) - 1
    right = from_behind(goal + 1, "bxy", -1) - 1
    numbers = jnp.arange(blocks, dtype=jnp.int32)

    def rank(going):
        return jnp.sum((going[None, :] & (numbers[None, :] < numbers[:, None])).astype(jnp.int32), axis=1)

    def reaching(whose, from_index):
        going = (whose // blocks == here) & (whose >= 0)
        hit = going[:, None] & (whose[:, None] - here * blocks == numbers[None, :])
        return jnp.any(hit, axis=0), jnp.sum(jnp.where(hit, from_index(going)[:, None], 0), axis=0)

    is_left, left_index = reaching(left, rank)
    is_right, right_index = reaching(right, rank)
    kind = jnp.where(is_left, 1, jnp.where(is_right, 2, 0))
    index = jnp.where(is_left, left_index, jnp.where(is_right, right_index, numbers))
    used = kind[None, :, None] == jnp.arange(3, dtype=jnp.int32)[:, None, None]
    before = used & (numbers[:, None] <= numbers[None, :])[None]
    latest = jnp.max(jnp.where(before, numbers[None, :, None], -1), axis=1)
    held = jnp.sum(jnp.where(numbers[None, :, None] == latest[:, None, :], index[None, :, None], 0), axis=1)
    table = jnp.concatenate([held, kind[None]], axis=0).astype(jnp.int32)

    way = jnp.where(goal // blocks == here + 1, 0, jnp.where(goal // blocks == here - 1, 1, 2))
    key = way * blocks + numbers
    place_of = jnp.sum((key[None, :] < key[:, None]).astype(jnp.int32), axis=1)
    rights = jnp.sum((way == 0).astype(jnp.int32))
    lefts = jnp.sum((way == 1).astype(jnp.int32))

    def in_order(values, positions):
        return jnp.sum(jnp.where(place_of[:, None] == positions[None, :], values[:, None], 0), axis=0)

    stays = jnp.minimum(jnp.maximum(numbers, rights + lefts), blocks - 1)
    plan = jnp.stack([
        in_order(numbers, numbers), in_order(way, numbers),
        jnp.minimum(numbers, jnp.maximum(rights - 1, 0)),
        jnp.maximum(jnp.minimum(numbers - rights, lefts - 1), 0),
        in_order(goal % blocks, stays),
    ]).astype(jnp.int32)
    return plan, table


def on_device(pdfs, relax, fluid, targets):
    q, blocks, rows, width = pdfs.shape
    edge = rows
    f32 = jnp.float32
    plan, table = routes_of(targets, blocks)
    here, row = lax.axis_index("bxy"), lax.axis_index("bz")
    ends = jnp.stack([here == 0, here == lax.axis_size("bxy") - 1, row == 0,
                      row == lax.axis_size("bz") - 1]).astype(jnp.int32)
    full = pl.BlockSpec((q, 1, rows, width), lambda s: (0, s, 0, 0))
    cell = pl.BlockSpec((1, rows, width), lambda s: (s, 0, 0))
    cell_below = pl.BlockSpec((1, rows, width), lambda s: (jnp.maximum(s - 1, 0), 0, 0))
    cell_above = pl.BlockSpec((1, rows, width), lambda s: (jnp.minimum(s + 1, blocks - 1), 0, 0))
    below = pl.BlockSpec((5, 1, rows, width), lambda s: (0, jnp.maximum(s - 1, 0), 0, 0))
    above = pl.BlockSpec((5, 1, rows, width), lambda s: (1, jnp.minimum(s + 1, blocks - 1), 0, 0))
    y_shape, x_shape, c_shape = (2, 6, rows, 128), (2, blocks, 8, width), (4, 8, 128)
    y_spec = pl.BlockSpec(y_shape, lambda s: (0, 0, 0, 0))
    x_all = pl.BlockSpec(x_shape, lambda s: (0, 0, 0, 0))
    x_spec = pl.BlockSpec((2, 1, 8, width), lambda s: (0, s, 0, 0))
    c_spec = pl.BlockSpec(c_shape, lambda s: (0, 0, 0))
    halo_out = [jax.ShapeDtypeStruct(s, f32) for s in (y_shape, x_shape, c_shape)]
    big = jax.ShapeDtypeStruct(pdfs.shape, f32)
    params = pltpu.CompilerParams(vmem_limit_bytes=VMEM_LIMIT)

    post, ys, xs, cs = pl.pallas_call(
        functools.partial(first_kernel, edge), grid=(blocks,),
        out_shape=[big] + halo_out, in_specs=[full, cell, cell],
        out_specs=[full, y_spec, x_spec, c_spec], compiler_params=params, name="first",
    )(pdfs, relax, fluid)
    halo = exchange(ys, xs, cs)
    post, mask, ys, xs, cs = pl.pallas_call(
        functools.partial(middle_kernel, edge), grid=(blocks,),
        out_shape=[big, jax.ShapeDtypeStruct(fluid.shape, jnp.int32)] + halo_out,
        in_specs=[pl.BlockSpec(memory_space=pltpu.SMEM), full, below, above, cell, cell, cell_below, cell_above,
                  y_spec, x_all, c_spec],
        out_specs=[full, cell, y_spec, x_spec, c_spec],
        scratch_shapes=[pltpu.VMEM((q, rows, width), f32)], compiler_params=params, name="middle",
    )(ends, post, post, post, relax, fluid, fluid, fluid, *halo)
    halo = exchange(ys, xs, cs)
    def moved(spec, shift):
        shape = spec.block_shape
        if len(shape) == 3:
            return pl.BlockSpec(shape, lambda g, plan: (plan[0, g], 0, 0))
        lead = 1 if shift == 1 else 0
        return pl.BlockSpec(
            shape, lambda g, plan: (lead, jnp.minimum(jnp.maximum(plan[0, g] + shift, 0), blocks - 1), 0, 0))

    def whole(shape):
        return pl.BlockSpec(shape, lambda g, plan: (0,) * len(shape))

    def out(row):
        return pl.BlockSpec((q, 1, rows, width), lambda g, plan: (0, plan[row, g], 0, 0))

    sent = jax.ShapeDtypeStruct((q, blocks // 2, rows, width), f32)
    right, left, kept = pl.pallas_call(
        functools.partial(last_kernel, edge), out_shape=[sent, sent, big],
        grid_spec=pltpu.PrefetchScalarGridSpec(
            num_scalar_prefetch=1, grid=(blocks,),
            in_specs=[moved(cell, 0), moved(full, 0), moved(below, -1), moved(above, 1),
                      whole(y_shape), whole(x_shape), whole(c_shape)],
            out_specs=[out(2), out(3), out(4)],
            scratch_shapes=[pltpu.VMEM((q, 1, rows, width), f32)]),
        compiler_params=params, name="last",
    )(plan, mask, post, post, post, *halo)
    from_left, from_right = migrate(right, left)
    return place(kept, from_left, from_right, table)


def solution(mesh):
    placed = (
        P(None, None, "bxy", "bz"),
        P(None, "bxy", "bz"),
        P(None, "bxy", "bz"),
        P("bz", "bxy", None),
    )
    return jax.shard_map(
        on_device, mesh=mesh, in_specs=placed, out_specs=P(None, None, "bxy", "bz"), check_vma=False
    )
```

```python
import functools
import math

import jax
import jax.numpy as jnp
from jax import lax
from jax.experimental import pallas as pl
from jax.experimental.pallas import tpu as pltpu
from jax.sharding import PartitionSpec as P

MESH = pl.DeviceIdType.MESH
VELOCITIES = (
    (0, 0, 0), (1, 0, 0), (-1, 0, 0), (0, 1, 0), (0, -1, 0), (0, 0, 1), (0, 0, -1),
    (1, 1, 0), (-1, -1, 0), (1, -1, 0), (-1, 1, 0), (1, 0, 1), (-1, 0, -1),
    (1, 0, -1), (-1, 0, 1), (0, 1, 1), (0, -1, -1), (0, 1, -1), (0, -1, 1),
)
OPPOSITE = (0, 2, 1, 4, 3, 6, 5, 8, 7, 10, 9, 12, 11, 14, 13, 16, 15, 18, 17)
Q = 19
ORDER = (5, 11, 14, 15, 18, 6, 12, 13, 16, 17, 0, 1, 2, 3, 4, 7, 8, 9, 10)
AT = tuple(ORDER.index(i) for i in range(Q))
NATURAL = tuple(range(Q))
Y_SENT = tuple(tuple(i for i in range(Q) if VELOCITIES[i][1] == c) for c in (1, -1))
X_SENT = tuple(tuple(i for i in range(Q) if VELOCITIES[i][0] == c) for c in (1, -1))
CORNERS = (7, 8, 9, 10)
SIDE = {1: 0, -1: 1}
VMEM_LIMIT = 60 * 1024 * 1024


def collide(f, rate):
    pair = {i: (f[i] + f[i + 1], f[i] - f[i + 1]) for i in range(1, Q, 2)}
    density = f[0]
    for i in range(1, Q, 2):
        density = density + pair[i][0]
    scale = 3.0 / density
    flow = []
    for axis in range(3):
        total = None
        for i in range(1, Q, 2):
            c = VELOCITIES[i][axis]
            if c:
                d = pair[i][1]
                total = d if total is None else (total + d if c == 1 else total - d)
        flow.append(total * scale)
    base = 1.0 - (flow[0] * flow[0] + flow[1] * flow[1] + flow[2] * flow[2]) * (1.0 / 6.0)
    keep = 1.0 - rate
    drive = rate * density
    post = [None] * Q
    post[0] = keep * f[0] + (drive * (1.0 / 3.0)) * base
    near, far = drive * (1.0 / 18.0), drive * (1.0 / 36.0)
    for i in range(1, Q, 2):
        along = None
        for axis in range(3):
            c = VELOCITIES[i][axis]
            if c:
                along = flow[axis] if along is None else (along + flow[axis] if c == 1 else along - flow[axis])
        even = base + 0.5 * (along * along)
        weight = near if i < 7 else far
        post[i] = keep * f[i] + weight * (even + along)
        post[i + 1] = keep * f[i + 1] + weight * (even - along)
    return post


def collide_block(read, relax_ref, fluid_ref, post_ref):
    rows, width = relax_ref.shape[1:]
    tiles = width // 128

    def body(step, carry):
        r = pl.multiple_of((step // tiles) * 8, 8)
        c = pl.multiple_of((step % tiles) * 128, 128)
        at = (pl.ds(r, 8), pl.ds(c, 128))
        rate = jnp.where(fluid_ref[(0,) + at] > 0, relax_ref[(0,) + at], 0.0)
        post = collide([read(i, at) for i in range(Q)], rate)
        for i in range(Q):
            post_ref[(AT[i], 0) + at] = post[i]
        return carry

    lax.fori_loop(0, (rows // 8) * tiles, body, 0, unroll=2)


def emit_halo(slot, last, edge, post_ref, fluid_ref, ys_ref, xs_ref, cs_ref):
    rows, width = fluid_ref.shape[1:]
    lane = lax.broadcasted_iota(jnp.int32, (rows, 128), 1)
    mine = lane // edge == slot
    for side, first in ((0, width - 128), (1, 0)):
        turn = slot * edge + (edge if side == 0 else 0)
        turn = lax.rem(turn, 128)
        for n in range(6):
            if n < 5:
                tile = post_ref[AT[Y_SENT[side][n]], 0, :, first:first + 128]
            else:
                tile = fluid_ref[0, :, first:first + 128].astype(jnp.float32)
            ys_ref[side, n] = jnp.where(mine, pltpu.roll(tile, turn, 1), ys_ref[side, n])
    for side, row in ((0, rows - 1), (1, 0)):
        for n in range(5):
            xs_ref[side, 0, n:n + 1, :] = post_ref[AT[X_SENT[side][n]], 0, row:row + 1, :]
        xs_ref[side, 0, 5:6, :] = fluid_ref[0, row:row + 1, :].astype(jnp.float32)
        xs_ref[side, 0, 6:8, :] = jnp.zeros((2, width), jnp.float32)

    @pl.when(last)
    def _():
        for k, i in enumerate(CORNERS):
            cx, cy, _z = VELOCITIES[i]
            row = rows - 1 if cx == 1 else 0
            ys = SIDE[cy]
            cs_ref[k, 0:1, :] = ys_ref[ys, Y_SENT[ys].index(i), row:row + 1, :]
            cs_ref[k, 1:2, :] = ys_ref[ys, 5, row:row + 1, :]
            cs_ref[k, 2:8, :] = jnp.zeros((6, 128), jnp.float32)


def first_kernel(edge, pdfs_ref, relax_ref, fluid_ref, post_ref, ys_ref, xs_ref, cs_ref):
    slot = pl.program_id(0)
    collide_block(lambda i, at: pdfs_ref[(i, 0) + at], relax_ref, fluid_ref, post_ref)
    emit_halo(slot, slot == pl.num_programs(0) - 1, edge, post_ref, fluid_ref, ys_ref, xs_ref, cs_ref)


def remote(src, dst, send_sem, recv_sem, device):
    return pltpu.make_async_remote_copy(
        src_ref=src, dst_ref=dst, send_sem=send_sem, recv_sem=recv_sem, device_id=device, device_id_type=MESH)


def halo_kernel(noted, *refs):
    ys, xs, cs = refs[:3]
    yr, xr, cr = refs[3 + noted:6 + noted]
    send_sem, recv_sem = refs[-2:]
    nz, nb = lax.axis_size("bz"), lax.axis_size("bxy")
    z, b = lax.axis_index("bz"), lax.axis_index("bxy")

    def there(dz, db):
        exists = None
        for at, step, count in ((z, dz, nz), (b, db, nb)):
            if step:
                inside = at < count - 1 if step == 1 else at > 0
                exists = inside if exists is None else exists & inside
        return exists

    routes = [(ys.at[0], yr.at[0], 1, 0), (ys.at[1], yr.at[1], -1, 0),
              (xs.at[0], xr.at[0], 0, 1), (xs.at[1], xr.at[1], 0, -1)]
    for k, i in enumerate(CORNERS):
        routes.append((cs.at[k], cr.at[k], VELOCITIES[i][1], VELOCITIES[i][0]))
    peers = [route[2:] for route in routes]
    if noted:
        note, from_left, from_right = refs[3], refs[7], refs[8]
        routes += [(note, from_left, 0, 1), (note, from_right, 0, -1)]
    barrier = pltpu.get_barrier_semaphore()
    count = 0
    for dz, db in peers:
        count = count + there(dz, db).astype(jnp.int32)

        @pl.when(there(dz, db))
        def _():
            pl.semaphore_signal(barrier, inc=1, device_id=(z + dz, b + db), device_id_type=MESH)

    pl.semaphore_wait(barrier, count)
    for n, (src, dst, dz, db) in enumerate(routes):
        @pl.when(there(dz, db))
        def _():
            remote(src, dst, send_sem.at[n], recv_sem.at[n], (z + dz, b + db)).start()

    for n, (src, dst, dz, db) in enumerate(routes):
        @pl.when(there(dz, db))
        def _():
            remote(src, dst, send_sem.at[n], recv_sem.at[n], (z + dz, b + db)).wait_send()

        @pl.when(there(-dz, -db))
        def _():
            remote(src, dst, send_sem.at[n], recv_sem.at[n], (z - dz, b - db)).wait_recv()


def exchange(ys, xs, cs, note=None):
    hbm = pl.BlockSpec(memory_space=pl.ANY)
    noted = note is not None
    sent = [ys, xs, cs] + ([note] if noted else [])
    got = sent + ([note] if noted else [])
    count = 8 + 2 * noted
    return pl.pallas_call(
        functools.partial(halo_kernel, int(noted)),
        out_shape=[jax.ShapeDtypeStruct(a.shape, a.dtype) for a in got],
        in_specs=[hbm] * len(sent),
        out_specs=[hbm] * len(got),
        scratch_shapes=[pltpu.SemaphoreType.DMA((count,)), pltpu.SemaphoreType.DMA((count,))],
        compiler_params=pltpu.CompilerParams(collective_id=0 if noted else 2, has_side_effects=True,
                                             vmem_limit_bytes=VMEM_LIMIT),
        name="halo_noted" if noted else "halo",
    )(*sent)


def lane_shift(velocity, slot, edge, here, below, above, beside):
    _cx, cy, cz = velocity
    width = here.shape[1]
    step = cy * edge + cz
    moved = here if step == 0 else pltpu.roll(here, step % width, 1)
    if cz:
        depth = lax.broadcasted_iota(jnp.int32, here.shape, 1) % edge
        other, face = (below, 0) if cz == 1 else (above, edge - 1)
        carry = step - cz * edge
        wrapped = other if carry == 0 else pltpu.roll(other, carry % width, 1)
        moved = jnp.where(depth == face, wrapped, moved)
    if cy:
        lane = lax.broadcasted_iota(jnp.int32, (here.shape[0], 128), 1)
        offset = 128 if cy == 1 else 256 - edge
        outside = pltpu.roll(beside, lax.rem(offset + cz + 128 - slot * edge, 128), 1)
        if cy == 1:
            moved = jnp.concatenate([jnp.where(lane < edge, outside, moved[:, :128]), moved[:, 128:]], axis=1)
        else:
            moved = jnp.concatenate(
                [moved[:, :-128], jnp.where(lane >= 128 - edge, outside, moved[:, -128:])], axis=1)
    return moved


def arrive(i, slot, edge, slots, here, below, above, yr_ref, xr_ref, cr_ref, fluid):
    velocity = cx, cy, cz = VELOCITIES[i]
    beside = None
    if cy:
        side = SIDE[cy]
        beside = yr_ref[side, 5 if fluid else Y_SENT[side].index(i)]
    moved = lane_shift(velocity, slot, edge, here, below, above, beside)
    if cx:
        side = SIDE[cx]
        row = 5 if fluid else X_SENT[side].index(i)
        rows = moved.shape[0]

        def plane(s):
            return jnp.broadcast_to(xr_ref[side, s, row:row + 1, :], (8, moved.shape[1]))

        corner = None
        if cy:
            k = CORNERS.index(i)
            n = 1 if fluid else 0
            corner = jnp.broadcast_to(cr_ref[k, n:n + 1, :], (8, 128))
        entering = lane_shift(
            velocity, slot, edge, plane(slot), plane(jnp.maximum(slot - 1, 0)) if cz == 1 else None,
            plane(jnp.minimum(slot + 1, slots - 1)) if cz == -1 else None, corner)
        index = lax.broadcasted_iota(jnp.int32, (8, moved.shape[1]), 0)
        moved = pltpu.roll(moved, cx % rows, 0)
        if cx == 1:
            moved = jnp.concatenate([jnp.where(index == 0, entering, moved[:8]), moved[8:]], axis=0)
        else:
            moved = jnp.concatenate([moved[:-8], jnp.where(index == 7, entering, moved[-8:])], axis=0)
    return moved


def stream_block(slot, edge, slots, mask_ref, post_ref, below_ref, above_ref, yr_ref, xr_ref, cr_ref, write):
    for i in range(Q):
        cz = VELOCITIES[i][2]
        own = post_ref[AT[i], 0]
        if i == 0:
            write(0, own)
            continue
        value = arrive(
            i, slot, edge, slots, own, below_ref[AT[i], 0] if cz == 1 else None,
            above_ref[AT[i] - 5, 0] if cz == -1 else None, yr_ref, xr_ref, cr_ref, False)
        mask = mask_ref[0]
        stay = jnp.where(mask > 0, post_ref[AT[OPPOSITE[i]], 0], own)
        write(i, jnp.where((mask & (1 << i)) != 0, value, stay))


def middle_kernel(edge, ends_ref, post_ref, below_ref, above_ref, relax_ref, fluid_ref, fbelow_ref, fabove_ref,
                  yr_ref, xr_ref, cr_ref, out_ref, mask_ref, ys_ref, xs_ref, cs_ref, next_ref):
    slot, slots = pl.program_id(0), pl.num_programs(0)
    rows, width = fluid_ref.shape[1:]
    row = lax.broadcasted_iota(jnp.int32, (rows, width), 0)
    lane = lax.broadcasted_iota(jnp.int32, (rows, width), 1)
    depth = lane % edge
    fluid = fluid_ref[0].astype(jnp.float32)
    bits = jnp.ones((rows, width), jnp.int32)
    for i in range(1, Q):
        cx, cy, cz = VELOCITIES[i]
        source = arrive(i, slot, edge, slots, fluid, fbelow_ref[0].astype(jnp.float32) if cz == 1 else None,
                        fabove_ref[0].astype(jnp.float32) if cz == -1 else None, yr_ref, xr_ref, cr_ref, True)
        bit = jnp.where(source > 0.5, 1 << i, 0)
        if cx:
            edge_row = 0 if cx == 1 else rows - 1
            bit = jnp.where((row == edge_row) & (ends_ref[0 if cx == 1 else 1] > 0), 0, bit)
        if cy:
            outer = lane < edge if cy == 1 else lane >= width - edge
            bit = jnp.where(outer & (ends_ref[2 if cy == 1 else 3] > 0), 0, bit)
        if cz:
            final = 0 if cz == 1 else slots - 1
            face = 0 if cz == 1 else edge - 1
            bit = jnp.where((depth == face) & (slot == final), 0, bit)
        bits = bits | bit
    mask_ref[0] = jnp.where(fluid_ref[0] > 0, bits, 0)

    def write(i, value):
        next_ref[i] = value

    stream_block(slot, edge, slots, mask_ref, post_ref, below_ref, above_ref, yr_ref, xr_ref, cr_ref, write)
    collide_block(lambda i, at: next_ref[(i,) + at], relax_ref, fluid_ref, out_ref)
    emit_halo(slot, slot == slots - 1, edge, out_ref, fluid_ref, ys_ref, xs_ref, cs_ref)


def last_kernel(edge, plan_ref, mask_ref, post_ref, below_ref, above_ref, yr_ref, xr_ref, cr_ref,
                right_ref, left_ref, kept_ref, next_ref):
    def write(i, value):
        next_ref[i, 0] = value

    g = pl.program_id(0)
    stream_block(plan_ref[0, g], edge, pl.num_programs(0), mask_ref, post_ref, below_ref, above_ref,
                 yr_ref, xr_ref, cr_ref, write)
    for kind, out_ref in enumerate((right_ref, left_ref, kept_ref)):
        @pl.when(plan_ref[1, g] == kind)
        def _():
            def copy(i, carry):
                out_ref[i] = next_ref[i]
                return carry

            lax.fori_loop(0, Q, copy, 0)


def migrate_kernel(right, left, from_left, from_right, passing, send_sem, recv_sem):
    nb = lax.axis_size("bxy")
    z, b = lax.axis_index("bz"), lax.axis_index("bxy")
    half = (Q + 1) // 2
    cuts = (0, half // 2, half, half + (Q - half + 1) // 2, Q)
    chunks = [(n, slice(cuts[n], cuts[n + 1]), n < 2) for n in range(4)]
    across = math.isqrt(nb // 2)
    row = 2 * across
    bends = across == 2 and nb == 2 * row
    cut = row - 1 if bends else nb
    low, high = cut + 1 - row, cut + row
    no = b < 0
    goes_right, goes_left = (b < nb - 1) & (b != cut), (b > 0) & (b != cut + 1)
    at_cut, past_cut, is_low, is_high = (
        (b == cut, b == cut + 1, b == low, b == high) if bends else (no, no, no, no))
    meets = [(goes_right, b + 1), (goes_left, b - 1)]
    if bends:
        for who in (at_cut, past_cut):
            meets += [(who, low), (who, high)]
        for who in (is_low, is_high):
            meets += [(who, cut), (who, cut + 1)]
    barrier = pltpu.get_barrier_semaphore()
    count = 0
    for who, peer in meets:
        count = count + who.astype(jnp.int32)

        @pl.when(who)
        def _():
            pl.semaphore_signal(barrier, inc=1, device_id=(z, peer), device_id_type=MESH)

    pl.semaphore_wait(barrier, count)

    def copy(src, dst, c, part, sent, got, peer):
        return remote(src.at[part], dst.at[part], send_sem.at[sent, c], recv_sem.at[got, c], (z, peer))

    for c, part, first in chunks:
        @pl.when(goes_right)
        def _():
            copy(right, from_left, c, part, 0, 0, b + 1).start()

        @pl.when(goes_left)
        def _():
            copy(left, from_right, c, part, 1, 1, b - 1).start()

        if bends:
            @pl.when(at_cut)
            def _():
                copy(right, passing, c, part, 0, 2, low if first else high).start()

            @pl.when(past_cut)
            def _():
                copy(left, passing, c, part, 1, 2, high if first else low).start()

    if bends:
        for who, ahead in ((is_low, True), (is_high, False)):
            @pl.when(who)
            def _():
                for n in (0, 2, 1, 3):
                    c, part, first = chunks[n]
                    copy(right, passing, c, part, 2, 2, cut).wait_recv()
                    if first == ahead:
                        copy(passing, from_left, c, part, 2, 0, cut + 1).start()
                    else:
                        copy(passing, from_right, c, part, 2, 1, cut).start()
                for c, part, first in chunks:
                    copy(passing, from_left, c, part, 2, 0, cut).wait_send()

    for c, part, first in chunks:
        @pl.when(b < nb - 1)
        def _():
            copy(right, from_left, c, part, 0, 0, b + 1).wait_send()
            copy(left, from_right, c, part, 1, 1, b + 1).wait_recv()

        @pl.when(b > 0)
        def _():
            copy(left, from_right, c, part, 1, 1, b - 1).wait_send()
            copy(right, from_left, c, part, 0, 0, b - 1).wait_recv()


def migrate(right, left):
    hbm = pl.BlockSpec(memory_space=pl.ANY)
    shape = jax.ShapeDtypeStruct(right.shape, right.dtype)
    from_left, from_right, _passing = pl.pallas_call(
        migrate_kernel, out_shape=[shape] * 3, in_specs=[hbm] * 2, out_specs=[hbm] * 3,
        scratch_shapes=[pltpu.SemaphoreType.DMA((3, 4)), pltpu.SemaphoreType.DMA((3, 4))],
        compiler_params=pltpu.CompilerParams(collective_id=1, has_side_effects=True, vmem_limit_bytes=VMEM_LIMIT),
        name="migrate",
    )(right, left)
    return from_left, from_right


def place_kernel(table_ref, final_ref, left_ref, right_ref, out_ref):
    kind = table_ref[3, pl.program_id(0)]

    @pl.when(kind == 0)
    def _():
        out_ref[...] = final_ref[...]

    @pl.when(kind == 1)
    def _():
        out_ref[...] = left_ref[...]

    @pl.when(kind == 2)
    def _():
        out_ref[...] = right_ref[...]


def place(final, left, right, table):
    q, blocks, rows, width = final.shape
    parts = 2 if rows % 16 == 0 else 1
    block = (q, 1, rows // parts, width)

    def taken(kind):
        return pl.BlockSpec(
            block, lambda k, h, table: (0, table[kind, k], jnp.where(table[3, k] == kind, h, parts - 1), 0))

    return pl.pallas_call(
        place_kernel,
        out_shape=jax.ShapeDtypeStruct(final.shape, final.dtype),
        grid_spec=pltpu.PrefetchScalarGridSpec(
            num_scalar_prefetch=1, grid=(blocks, parts),
            in_specs=[taken(0), taken(1), taken(2)],
            out_specs=pl.BlockSpec(block, lambda k, h, table: (0, k, h, 0))),
        compiler_params=pltpu.CompilerParams(vmem_limit_bytes=VMEM_LIMIT),
        name="place",
    )(table, final, left, right)


def arrivals(goal, left, right):
    blocks = goal.shape[0]
    here, owners = lax.axis_index("bxy"), lax.axis_size("bxy")
    numbers = jnp.arange(blocks, dtype=jnp.int32)

    def rank(going):
        return jnp.sum((going[None, :] & (numbers[None, :] < numbers[:, None])).astype(jnp.int32), axis=1)

    def reaching(whose, valid, from_index):
        going = (whose // blocks == here) & valid
        hit = going[:, None] & (whose[:, None] - here * blocks == numbers[None, :])
        return jnp.any(hit, axis=0), jnp.sum(jnp.where(hit, from_index(going)[:, None], 0), axis=0)

    is_left, left_index = reaching(left, here > 0, rank)
    is_right, right_index = reaching(right, here < owners - 1, rank)
    kind = jnp.where(is_left, 1, jnp.where(is_right, 2, 0))
    index = jnp.where(is_left, left_index, jnp.where(is_right, right_index, numbers))
    used = kind[None, :, None] == jnp.arange(3, dtype=jnp.int32)[:, None, None]
    before = used & (numbers[:, None] <= numbers[None, :])[None]
    latest = jnp.max(jnp.where(before, numbers[None, :, None], -1), axis=1)
    held = jnp.sum(jnp.where(numbers[None, :, None] == latest[:, None, :], index[None, :, None], 0), axis=1)
    return jnp.concatenate([held, kind[None]], axis=0).astype(jnp.int32)


def departures(goal):
    blocks = goal.shape[0]
    here = lax.axis_index("bxy")
    numbers = jnp.arange(blocks, dtype=jnp.int32)
    way = jnp.where(goal // blocks == here + 1, 0, jnp.where(goal // blocks == here - 1, 1, 2))
    key = way * blocks + numbers
    place_of = jnp.sum((key[None, :] < key[:, None]).astype(jnp.int32), axis=1)
    rights = jnp.sum((way == 0).astype(jnp.int32))
    lefts = jnp.sum((way == 1).astype(jnp.int32))

    def in_order(values, positions):
        return jnp.sum(jnp.where(place_of[:, None] == positions[None, :], values[:, None], 0), axis=0)

    stays = jnp.minimum(jnp.maximum(numbers, rights + lefts), blocks - 1)
    return jnp.stack([
        in_order(numbers, numbers), in_order(way, numbers),
        jnp.minimum(numbers, jnp.maximum(rights - 1, 0)),
        jnp.maximum(jnp.minimum(numbers - rights, lefts - 1), 0),
        in_order(goal % blocks, stays),
    ]).astype(jnp.int32)


def on_device(pdfs, relax, fluid, targets):
    q, blocks, rows, width = pdfs.shape
    edge = rows
    f32 = jnp.float32
    goal = targets.reshape((blocks,))
    plan = departures(goal)
    note = jnp.broadcast_to(jnp.pad(goal, (0, 128 - blocks))[None], (8, 128))
    here, row = lax.axis_index("bxy"), lax.axis_index("bz")
    ends = jnp.stack([here == 0, here == lax.axis_size("bxy") - 1, row == 0,
                      row == lax.axis_size("bz") - 1]).astype(jnp.int32)
    full = pl.BlockSpec((q, 1, rows, width), lambda s: (0, s, 0, 0))
    cell = pl.BlockSpec((1, rows, width), lambda s: (s, 0, 0))
    cell_below = pl.BlockSpec((1, rows, width), lambda s: (jnp.maximum(s - 1, 0), 0, 0))
    cell_above = pl.BlockSpec((1, rows, width), lambda s: (jnp.minimum(s + 1, blocks - 1), 0, 0))
    below = pl.BlockSpec((5, 1, rows, width), lambda s: (0, jnp.maximum(s - 1, 0), 0, 0))
    above = pl.BlockSpec((5, 1, rows, width), lambda s: (1, jnp.minimum(s + 1, blocks - 1), 0, 0))
    y_shape, x_shape, c_shape = (2, 6, rows, 128), (2, blocks, 8, width), (4, 8, 128)
    y_spec = pl.BlockSpec(y_shape, lambda s: (0, 0, 0, 0))
    x_all = pl.BlockSpec(x_shape, lambda s: (0, 0, 0, 0))
    x_spec = pl.BlockSpec((2, 1, 8, width), lambda s: (0, s, 0, 0))
    c_spec = pl.BlockSpec(c_shape, lambda s: (0, 0, 0))
    halo_out = [jax.ShapeDtypeStruct(s, f32) for s in (y_shape, x_shape, c_shape)]
    big = jax.ShapeDtypeStruct(pdfs.shape, f32)
    params = pltpu.CompilerParams(vmem_limit_bytes=VMEM_LIMIT)

    post, ys, xs, cs = pl.pallas_call(
        functools.partial(first_kernel, edge), grid=(blocks,),
        out_shape=[big] + halo_out, in_specs=[full, cell, cell],
        out_specs=[full, y_spec, x_spec, c_spec], compiler_params=params, name="first",
    )(pdfs, relax, fluid)
    *halo, left_goal, right_goal = exchange(ys, xs, cs, note)
    post, mask, ys, xs, cs = pl.pallas_call(
        functools.partial(middle_kernel, edge), grid=(blocks,),
        out_shape=[big, jax.ShapeDtypeStruct(fluid.shape, jnp.int32)] + halo_out,
        in_specs=[pl.BlockSpec(memory_space=pltpu.SMEM), full, below, above, cell, cell, cell_below, cell_above,
                  y_spec, x_all, c_spec],
        out_specs=[full, cell, y_spec, x_spec, c_spec],
        scratch_shapes=[pltpu.VMEM((q, rows, width), f32)], compiler_params=params, name="middle",
    )(ends, post, post, post, relax, fluid, fluid, fluid, *halo)
    halo = exchange(ys, xs, cs)
    def moved(spec, shift):
        shape = spec.block_shape
        if len(shape) == 3:
            return pl.BlockSpec(shape, lambda g, plan: (plan[0, g], 0, 0))
        lead = 1 if shift == 1 else 0
        return pl.BlockSpec(
            shape, lambda g, plan: (lead, jnp.minimum(jnp.maximum(plan[0, g] + shift, 0), blocks - 1), 0, 0))

    def whole(shape):
        return pl.BlockSpec(shape, lambda g, plan: (0,) * len(shape))

    def out(row):
        return pl.BlockSpec((q, 1, rows, width), lambda g, plan: (0, plan[row, g], 0, 0))

    sent = jax.ShapeDtypeStruct((q, blocks // 2, rows, width), f32)
    right, left, kept = pl.pallas_call(
        functools.partial(last_kernel, edge), out_shape=[sent, sent, big],
        grid_spec=pltpu.PrefetchScalarGridSpec(
            num_scalar_prefetch=1, grid=(blocks,),
            in_specs=[moved(cell, 0), moved(full, 0), moved(below, -1), moved(above, 1),
                      whole(y_shape), whole(x_shape), whole(c_shape)],
            out_specs=[out(2), out(3), out(4)],
            scratch_shapes=[pltpu.VMEM((q, 1, rows, width), f32)]),
        compiler_params=params, name="last",
    )(plan, mask, post, post, post, *halo)
    from_left, from_right = migrate(right, left)
    table = arrivals(goal, left_goal[0, :blocks], right_goal[0, :blocks])
    return place(kept, from_left, from_right, table)


def solution(mesh):
    placed = (
        P(None, None, "bxy", "bz"),
        P(None, "bxy", "bz"),
        P(None, "bxy", "bz"),
        P("bz", "bxy", None),
    )
    return jax.shard_map(
        on_device, mesh=mesh, in_specs=placed, out_specs=P(None, None, "bxy", "bz"), check_vma=False
    )
```

```python
import functools
import math

import jax
import jax.numpy as jnp
from jax import lax
from jax.experimental import pallas as pl
from jax.experimental.pallas import tpu as pltpu
from jax.sharding import PartitionSpec as P

MESH = pl.DeviceIdType.MESH
VELOCITIES = (
    (0, 0, 0), (1, 0, 0), (-1, 0, 0), (0, 1, 0), (0, -1, 0), (0, 0, 1), (0, 0, -1),
    (1, 1, 0), (-1, -1, 0), (1, -1, 0), (-1, 1, 0), (1, 0, 1), (-1, 0, -1),
    (1, 0, -1), (-1, 0, 1), (0, 1, 1), (0, -1, -1), (0, 1, -1), (0, -1, 1),
)
OPPOSITE = (0, 2, 1, 4, 3, 6, 5, 8, 7, 10, 9, 12, 11, 14, 13, 16, 15, 18, 17)
Q = 19
ORDER = (5, 11, 14, 15, 18, 6, 12, 13, 16, 17, 0, 1, 2, 3, 4, 7, 8, 9, 10)
AT = tuple(ORDER.index(i) for i in range(Q))
NATURAL = tuple(range(Q))
Y_SENT = tuple(tuple(i for i in range(Q) if VELOCITIES[i][1] == c) for c in (1, -1))
X_SENT = tuple(tuple(i for i in range(Q) if VELOCITIES[i][0] == c) for c in (1, -1))
CORNERS = (7, 8, 9, 10)
SIDE = {1: 0, -1: 1}
VMEM_LIMIT = 60 * 1024 * 1024


def collide(f, rate):
    pair = {i: (f[i] + f[i + 1], f[i] - f[i + 1]) for i in range(1, Q, 2)}
    density = f[0]
    for i in range(1, Q, 2):
        density = density + pair[i][0]
    scale = 3.0 / density
    flow = []
    for axis in range(3):
        total = None
        for i in range(1, Q, 2):
            c = VELOCITIES[i][axis]
            if c:
                d = pair[i][1]
                total = d if total is None else (total + d if c == 1 else total - d)
        flow.append(total * scale)
    base = 1.0 - (flow[0] * flow[0] + flow[1] * flow[1] + flow[2] * flow[2]) * (1.0 / 6.0)
    keep = 1.0 - rate
    drive = rate * density
    post = [None] * Q
    post[0] = keep * f[0] + (drive * (1.0 / 3.0)) * base
    near, far = drive * (1.0 / 18.0), drive * (1.0 / 36.0)
    for i in range(1, Q, 2):
        along = None
        for axis in range(3):
            c = VELOCITIES[i][axis]
            if c:
                along = flow[axis] if along is None else (along + flow[axis] if c == 1 else along - flow[axis])
        even = base + 0.5 * (along * along)
        weight = near if i < 7 else far
        post[i] = keep * f[i] + weight * (even + along)
        post[i + 1] = keep * f[i + 1] + weight * (even - along)
    return post


def collide_block(read, relax_ref, fluid_ref, post_ref):
    rows, width = relax_ref.shape[1:]
    tiles = width // 128

    def body(step, carry):
        r = pl.multiple_of((step // tiles) * 8, 8)
        c = pl.multiple_of((step % tiles) * 128, 128)
        at = (pl.ds(r, 8), pl.ds(c, 128))
        rate = jnp.where(fluid_ref[(0,) + at] > 0, relax_ref[(0,) + at], 0.0)
        post = collide([read(i, at) for i in range(Q)], rate)
        for i in range(Q):
            post_ref[(AT[i], 0) + at] = post[i]
        return carry

    lax.fori_loop(0, (rows // 8) * tiles, body, 0, unroll=2)


def emit_halo(slot, last, edge, post_ref, fluid_ref, ys_ref, xs_ref, cs_ref):
    rows, width = fluid_ref.shape[1:]
    lane = lax.broadcasted_iota(jnp.int32, (rows, 128), 1)
    mine = lane // edge == slot
    for side, first in ((0, width - 128), (1, 0)):
        turn = slot * edge + (edge if side == 0 else 0)
        turn = lax.rem(turn, 128)
        for n in range(6):
            if n < 5:
                tile = post_ref[AT[Y_SENT[side][n]], 0, :, first:first + 128]
            else:
                tile = fluid_ref[0, :, first:first + 128].astype(jnp.float32)
            ys_ref[side, n] = jnp.where(mine, pltpu.roll(tile, turn, 1), ys_ref[side, n])
    for side, row in ((0, rows - 1), (1, 0)):
        for n in range(5):
            xs_ref[side, 0, n:n + 1, :] = post_ref[AT[X_SENT[side][n]], 0, row:row + 1, :]
        xs_ref[side, 0, 5:6, :] = fluid_ref[0, row:row + 1, :].astype(jnp.float32)
        xs_ref[side, 0, 6:8, :] = jnp.zeros((2, width), jnp.float32)

    @pl.when(last)
    def _():
        for k, i in enumerate(CORNERS):
            cx, cy, _z = VELOCITIES[i]
            row = rows - 1 if cx == 1 else 0
            ys = SIDE[cy]
            cs_ref[k, 0:1, :] = ys_ref[ys, Y_SENT[ys].index(i), row:row + 1, :]
            cs_ref[k, 1:2, :] = ys_ref[ys, 5, row:row + 1, :]
            cs_ref[k, 2:8, :] = jnp.zeros((6, 128), jnp.float32)


def first_kernel(edge, pdfs_ref, relax_ref, fluid_ref, post_ref, ys_ref, xs_ref, cs_ref):
    slot = pl.program_id(0)
    collide_block(lambda i, at: pdfs_ref[(i, 0) + at], relax_ref, fluid_ref, post_ref)
    emit_halo(slot, slot == pl.num_programs(0) - 1, edge, post_ref, fluid_ref, ys_ref, xs_ref, cs_ref)


def remote(src, dst, send_sem, recv_sem, device):
    return pltpu.make_async_remote_copy(
        src_ref=src, dst_ref=dst, send_sem=send_sem, recv_sem=recv_sem, device_id=device, device_id_type=MESH)


def halo_kernel(noted, *refs):
    ys, xs, cs = refs[:3]
    yr, xr, cr = refs[3 + noted:6 + noted]
    send_sem, recv_sem = refs[-2:]
    nz, nb = lax.axis_size("bz"), lax.axis_size("bxy")
    z, b = lax.axis_index("bz"), lax.axis_index("bxy")

    def there(dz, db):
        exists = None
        for at, step, count in ((z, dz, nz), (b, db, nb)):
            if step:
                inside = at < count - 1 if step == 1 else at > 0
                exists = inside if exists is None else exists & inside
        return exists

    routes = [(ys.at[0], yr.at[0], 1, 0), (ys.at[1], yr.at[1], -1, 0),
              (xs.at[0], xr.at[0], 0, 1), (xs.at[1], xr.at[1], 0, -1)]
    for k, i in enumerate(CORNERS):
        routes.append((cs.at[k], cr.at[k], VELOCITIES[i][1], VELOCITIES[i][0]))
    peers = [route[2:] for route in routes]
    if noted:
        note, from_left, from_right = refs[3], refs[7], refs[8]
        routes += [(note, from_left, 0, 1), (note, from_right, 0, -1)]
    barrier = pltpu.get_barrier_semaphore()
    count = 0
    for dz, db in peers:
        count = count + there(dz, db).astype(jnp.int32)

        @pl.when(there(dz, db))
        def _():
            pl.semaphore_signal(barrier, inc=1, device_id=(z + dz, b + db), device_id_type=MESH)

    pl.semaphore_wait(barrier, count)
    for n, (src, dst, dz, db) in enumerate(routes):
        @pl.when(there(dz, db))
        def _():
            remote(src, dst, send_sem.at[n], recv_sem.at[n], (z + dz, b + db)).start()

    for n, (src, dst, dz, db) in enumerate(routes):
        @pl.when(there(dz, db))
        def _():
            remote(src, dst, send_sem.at[n], recv_sem.at[n], (z + dz, b + db)).wait_send()

        @pl.when(there(-dz, -db))
        def _():
            remote(src, dst, send_sem.at[n], recv_sem.at[n], (z - dz, b - db)).wait_recv()


def exchange(ys, xs, cs, note=None):
    hbm = pl.BlockSpec(memory_space=pl.ANY)
    noted = note is not None
    sent = [ys, xs, cs] + ([note] if noted else [])
    got = sent + ([note] if noted else [])
    count = 8 + 2 * noted
    return pl.pallas_call(
        functools.partial(halo_kernel, int(noted)),
        out_shape=[jax.ShapeDtypeStruct(a.shape, a.dtype) for a in got],
        in_specs=[hbm] * len(sent),
        out_specs=[hbm] * len(got),
        scratch_shapes=[pltpu.SemaphoreType.DMA((count,)), pltpu.SemaphoreType.DMA((count,))],
        compiler_params=pltpu.CompilerParams(collective_id=0 if noted else 2, has_side_effects=True,
                                             vmem_limit_bytes=VMEM_LIMIT),
        name="halo_noted" if noted else "halo",
    )(*sent)


def lane_shift(velocity, slot, edge, here, below, above, beside):
    _cx, cy, cz = velocity
    width = here.shape[1]
    step = cy * edge + cz
    moved = here if step == 0 else pltpu.roll(here, step % width, 1)
    if cz:
        depth = lax.broadcasted_iota(jnp.int32, here.shape, 1) % edge
        other, face = (below, 0) if cz == 1 else (above, edge - 1)
        carry = step - cz * edge
        wrapped = other if carry == 0 else pltpu.roll(other, carry % width, 1)
        moved = jnp.where(depth == face, wrapped, moved)
    if cy:
        lane = lax.broadcasted_iota(jnp.int32, (here.shape[0], 128), 1)
        offset = 128 if cy == 1 else 256 - edge
        outside = pltpu.roll(beside, lax.rem(offset + cz + 128 - slot * edge, 128), 1)
        if cy == 1:
            moved = jnp.concatenate([jnp.where(lane < edge, outside, moved[:, :128]), moved[:, 128:]], axis=1)
        else:
            moved = jnp.concatenate(
                [moved[:, :-128], jnp.where(lane >= 128 - edge, outside, moved[:, -128:])], axis=1)
    return moved


def arrive(i, slot, edge, slots, here, below, above, yr_ref, xr_ref, cr_ref, fluid):
    velocity = cx, cy, cz = VELOCITIES[i]
    beside = None
    if cy:
        side = SIDE[cy]
        beside = yr_ref[side, 5 if fluid else Y_SENT[side].index(i)]
    moved = lane_shift(velocity, slot, edge, here, below, above, beside)
    if cx:
        side = SIDE[cx]
        row = 5 if fluid else X_SENT[side].index(i)
        rows = moved.shape[0]

        def plane(s):
            return jnp.broadcast_to(xr_ref[side, s, row:row + 1, :], (8, moved.shape[1]))

        corner = None
        if cy:
            k = CORNERS.index(i)
            n = 1 if fluid else 0
            corner = jnp.broadcast_to(cr_ref[k, n:n + 1, :], (8, 128))
        entering = lane_shift(
            velocity, slot, edge, plane(slot), plane(jnp.maximum(slot - 1, 0)) if cz == 1 else None,
            plane(jnp.minimum(slot + 1, slots - 1)) if cz == -1 else None, corner)
        index = lax.broadcasted_iota(jnp.int32, (8, moved.shape[1]), 0)
        moved = pltpu.roll(moved, cx % rows, 0)
        if cx == 1:
            moved = jnp.concatenate([jnp.where(index == 0, entering, moved[:8]), moved[8:]], axis=0)
        else:
            moved = jnp.concatenate([moved[:-8], jnp.where(index == 7, entering, moved[-8:])], axis=0)
    return moved


def stream_block(slot, edge, slots, mask_ref, post_ref, below_ref, above_ref, yr_ref, xr_ref, cr_ref, write):
    for i in range(Q):
        cz = VELOCITIES[i][2]
        own = post_ref[AT[i], 0]
        if i == 0:
            write(0, own)
            continue
        value = arrive(
            i, slot, edge, slots, own, below_ref[AT[i], 0] if cz == 1 else None,
            above_ref[AT[i] - 5, 0] if cz == -1 else None, yr_ref, xr_ref, cr_ref, False)
        mask = mask_ref[0]
        stay = jnp.where(mask > 0, post_ref[AT[OPPOSITE[i]], 0], own)
        write(i, jnp.where((mask & (1 << i)) != 0, value, stay))


def middle_kernel(edge, post_ref, below_ref, above_ref, relax_ref, fluid_ref, fbelow_ref, fabove_ref,
                  yr_ref, xr_ref, cr_ref, out_ref, mask_ref, ys_ref, xs_ref, cs_ref, next_ref):
    slot, slots = pl.program_id(0), pl.num_programs(0)
    rows, width = fluid_ref.shape[1:]
    row = lax.broadcasted_iota(jnp.int32, (rows, width), 0)
    lane = lax.broadcasted_iota(jnp.int32, (rows, width), 1)
    depth = lane % edge
    z, b = lax.axis_index("bz"), lax.axis_index("bxy")
    at_end = (b == 0, b == lax.axis_size("bxy") - 1, z == 0, z == lax.axis_size("bz") - 1)
    fluid = fluid_ref[0].astype(jnp.float32)
    bits = jnp.ones((rows, width), jnp.int32)
    for i in range(1, Q):
        cx, cy, cz = VELOCITIES[i]
        source = arrive(i, slot, edge, slots, fluid, fbelow_ref[0].astype(jnp.float32) if cz == 1 else None,
                        fabove_ref[0].astype(jnp.float32) if cz == -1 else None, yr_ref, xr_ref, cr_ref, True)
        bit = jnp.where(source > 0.5, 1 << i, 0)
        if cx:
            edge_row = 0 if cx == 1 else rows - 1
            bit = jnp.where((row == edge_row) & at_end[0 if cx == 1 else 1], 0, bit)
        if cy:
            outer = lane < edge if cy == 1 else lane >= width - edge
            bit = jnp.where(outer & at_end[2 if cy == 1 else 3], 0, bit)
        if cz:
            final = 0 if cz == 1 else slots - 1
            face = 0 if cz == 1 else edge - 1
            bit = jnp.where((depth == face) & (slot == final), 0, bit)
        bits = bits | bit
    mask_ref[0] = jnp.where(fluid_ref[0] > 0, bits, 0)

    def write(i, value):
        next_ref[i] = value

    stream_block(slot, edge, slots, mask_ref, post_ref, below_ref, above_ref, yr_ref, xr_ref, cr_ref, write)
    collide_block(lambda i, at: next_ref[(i,) + at], relax_ref, fluid_ref, out_ref)
    emit_halo(slot, slot == slots - 1, edge, out_ref, fluid_ref, ys_ref, xs_ref, cs_ref)


def last_kernel(edge, plan_ref, mask_ref, post_ref, below_ref, above_ref, yr_ref, xr_ref, cr_ref,
                right_ref, left_ref, kept_ref, next_ref):
    def write(i, value):
        next_ref[i, 0] = value

    g = pl.program_id(0)
    stream_block(plan_ref[0, g], edge, pl.num_programs(0), mask_ref, post_ref, below_ref, above_ref,
                 yr_ref, xr_ref, cr_ref, write)
    for kind, out_ref in enumerate((right_ref, left_ref, kept_ref)):
        @pl.when(plan_ref[1, g] == kind)
        def _():
            def copy(i, carry):
                out_ref[i] = next_ref[i]
                return carry

            lax.fori_loop(0, Q, copy, 0)


def migrate_kernel(right, left, from_left, from_right, passing, send_sem, recv_sem):
    nb = lax.axis_size("bxy")
    z, b = lax.axis_index("bz"), lax.axis_index("bxy")
    half = (Q + 1) // 2
    cuts = (0, half // 2, half, half + (Q - half + 1) // 2, Q)
    chunks = [(n, slice(cuts[n], cuts[n + 1]), n < 2) for n in range(4)]
    across = math.isqrt(nb // 2)
    row = 2 * across
    bends = across == 2 and nb == 2 * row
    cut = row - 1 if bends else nb
    low, high = cut + 1 - row, cut + row
    no = b < 0
    goes_right, goes_left = (b < nb - 1) & (b != cut), (b > 0) & (b != cut + 1)
    at_cut, past_cut, is_low, is_high = (
        (b == cut, b == cut + 1, b == low, b == high) if bends else (no, no, no, no))
    meets = [(goes_right, b + 1), (goes_left, b - 1)]
    if bends:
        for who in (at_cut, past_cut):
            meets += [(who, low), (who, high)]
        for who in (is_low, is_high):
            meets += [(who, cut), (who, cut + 1)]
    barrier = pltpu.get_barrier_semaphore()
    count = 0
    for who, peer in meets:
        count = count + who.astype(jnp.int32)

        @pl.when(who)
        def _():
            pl.semaphore_signal(barrier, inc=1, device_id=(z, peer), device_id_type=MESH)

    pl.semaphore_wait(barrier, count)

    def copy(src, dst, c, part, sent, got, peer):
        return remote(src.at[part], dst.at[part], send_sem.at[sent, c], recv_sem.at[got, c], (z, peer))

    for c, part, first in chunks:
        @pl.when(goes_right)
        def _():
            copy(right, from_left, c, part, 0, 0, b + 1).start()

        @pl.when(goes_left)
        def _():
            copy(left, from_right, c, part, 1, 1, b - 1).start()

        if bends:
            @pl.when(at_cut)
            def _():
                copy(right, passing, c, part, 0, 2, low if first else high).start()

            @pl.when(past_cut)
            def _():
                copy(left, passing, c, part, 1, 2, high if first else low).start()

    if bends:
        for who, ahead in ((is_low, True), (is_high, False)):
            @pl.when(who)
            def _():
                for n in (0, 2, 1, 3):
                    c, part, first = chunks[n]
                    copy(right, passing, c, part, 2, 2, cut).wait_recv()
                    if first == ahead:
                        copy(passing, from_left, c, part, 2, 0, cut + 1).start()
                    else:
                        copy(passing, from_right, c, part, 2, 1, cut).start()
                for c, part, first in chunks:
                    copy(passing, from_left, c, part, 2, 0, cut).wait_send()

    for c, part, first in chunks:
        @pl.when(b < nb - 1)
        def _():
            copy(right, from_left, c, part, 0, 0, b + 1).wait_send()
            copy(left, from_right, c, part, 1, 1, b + 1).wait_recv()

        @pl.when(b > 0)
        def _():
            copy(left, from_right, c, part, 1, 1, b - 1).wait_send()
            copy(right, from_left, c, part, 0, 0, b - 1).wait_recv()


def migrate(right, left):
    hbm = pl.BlockSpec(memory_space=pl.ANY)
    shape = jax.ShapeDtypeStruct(right.shape, right.dtype)
    from_left, from_right, _passing = pl.pallas_call(
        migrate_kernel, out_shape=[shape] * 3, in_specs=[hbm] * 2, out_specs=[hbm] * 3,
        scratch_shapes=[pltpu.SemaphoreType.DMA((3, 4)), pltpu.SemaphoreType.DMA((3, 4))],
        compiler_params=pltpu.CompilerParams(collective_id=1, has_side_effects=True, vmem_limit_bytes=VMEM_LIMIT),
        name="migrate",
    )(right, left)
    return from_left, from_right


def place_kernel(table_ref, final_ref, left_ref, right_ref, out_ref):
    kind = table_ref[3, pl.program_id(0)]

    @pl.when(kind == 0)
    def _():
        out_ref[...] = final_ref[...]

    @pl.when(kind == 1)
    def _():
        out_ref[...] = left_ref[...]

    @pl.when(kind == 2)
    def _():
        out_ref[...] = right_ref[...]


def place(final, left, right, table):
    q, blocks, rows, width = final.shape
    parts = 1
    block = (q, 1, rows // parts, width)

    def taken(kind):
        return pl.BlockSpec(
            block, lambda k, h, table: (0, table[kind, k], jnp.where(table[3, k] == kind, h, parts - 1), 0))

    return pl.pallas_call(
        place_kernel,
        out_shape=jax.ShapeDtypeStruct(final.shape, final.dtype),
        grid_spec=pltpu.PrefetchScalarGridSpec(
            num_scalar_prefetch=1, grid=(blocks, parts),
            in_specs=[taken(0), taken(1), taken(2)],
            out_specs=pl.BlockSpec(block, lambda k, h, table: (0, k, h, 0))),
        compiler_params=pltpu.CompilerParams(vmem_limit_bytes=VMEM_LIMIT),
        name="place",
    )(table, final, left, right)


def tables_kernel(goal_ref, left_ref, right_ref, plan_ref, table_ref):
    here, owners = lax.axis_index("bxy"), lax.axis_size("bxy")
    blocks = goal_ref.shape[2]
    base = here * blocks

    def total(terms):
        return sum(t.astype(jnp.int32) for t in terms)

    goal = [goal_ref[0, 0, j] for j in range(blocks)]
    way = [jnp.where(g >= base + blocks, 0, jnp.where(g < base, 1, 2)) for g in goal]
    key = [way[j] * blocks + j for j in range(blocks)]
    at = [total(key[k] < key[j] for k in range(blocks)) for j in range(blocks)]
    rights, lefts = total(w == 0 for w in way), total(w == 1 for w in way)

    def in_order(values, position):
        return sum(jnp.where(at[j] == position, values[j], 0) for j in range(blocks))

    for g in range(blocks):
        plan_ref[0, g] = in_order(list(range(blocks)), g)
        plan_ref[1, g] = in_order(way, g)
        plan_ref[2, g] = jnp.minimum(g, jnp.maximum(rights - 1, 0))
        plan_ref[3, g] = jnp.maximum(jnp.minimum(g - rights, lefts - 1), 0)
        first = jnp.minimum(jnp.maximum(g, rights + lefts), blocks - 1)
        plan_ref[4, g] = in_order([lax.rem(v, blocks) for v in goal], first)

    kind = [jnp.int32(0)] * blocks
    index = [jnp.int32(k) for k in range(blocks)]
    for source, ref, valid in ((1, left_ref, here > 0), (2, right_ref, here < owners - 1)):
        rank = jnp.int32(0)
        for j in range(blocks):
            value = ref[j, 0]
            for k in range(blocks):
                hit = valid & (value == base + k)
                kind[k] = jnp.where(hit, source, kind[k])
                index[k] = jnp.where(hit, rank, index[k])
            rank = rank + (valid & (value >= base) & (value < base + blocks)).astype(jnp.int32)
    for source in range(3):
        held = jnp.int32(0)
        for k in range(blocks):
            held = jnp.where(kind[k] == source, index[k], held)
            table_ref[source, k] = held
    for k in range(blocks):
        table_ref[3, k] = kind[k]


def tables(targets, left_goal, right_goal):
    blocks = targets.shape[2]
    smem = pl.BlockSpec(memory_space=pltpu.SMEM)
    return pl.pallas_call(
        tables_kernel,
        out_shape=[jax.ShapeDtypeStruct((5, blocks), jnp.int32), jax.ShapeDtypeStruct((4, blocks), jnp.int32)],
        in_specs=[smem] * 3, out_specs=[smem] * 2, name="tables",
    )(targets, left_goal, right_goal)


def on_device(pdfs, relax, fluid, targets):
    q, blocks, rows, width = pdfs.shape
    edge = rows
    f32 = jnp.float32
    note = jnp.broadcast_to(targets.reshape((blocks, 1)), (blocks, 128))
    full = pl.BlockSpec((q, 1, rows, width), lambda s: (0, s, 0, 0))
    cell = pl.BlockSpec((1, rows, width), lambda s: (s, 0, 0))
    cell_below = pl.BlockSpec((1, rows, width), lambda s: (jnp.maximum(s - 1, 0), 0, 0))
    cell_above = pl.BlockSpec((1, rows, width), lambda s: (jnp.minimum(s + 1, blocks - 1), 0, 0))
    below = pl.BlockSpec((5, 1, rows, width), lambda s: (0, jnp.maximum(s - 1, 0), 0, 0))
    above = pl.BlockSpec((5, 1, rows, width), lambda s: (1, jnp.minimum(s + 1, blocks - 1), 0, 0))
    y_shape, x_shape, c_shape = (2, 6, rows, 128), (2, blocks, 8, width), (4, 8, 128)
    y_spec = pl.BlockSpec(y_shape, lambda s: (0, 0, 0, 0))
    x_all = pl.BlockSpec(x_shape, lambda s: (0, 0, 0, 0))
    x_spec = pl.BlockSpec((2, 1, 8, width), lambda s: (0, s, 0, 0))
    c_spec = pl.BlockSpec(c_shape, lambda s: (0, 0, 0))
    halo_out = [jax.ShapeDtypeStruct(s, f32) for s in (y_shape, x_shape, c_shape)]
    big = jax.ShapeDtypeStruct(pdfs.shape, f32)
    params = pltpu.CompilerParams(vmem_limit_bytes=VMEM_LIMIT)

    post, ys, xs, cs = pl.pallas_call(
        functools.partial(first_kernel, edge), grid=(blocks,),
        out_shape=[big] + halo_out, in_specs=[full, cell, cell],
        out_specs=[full, y_spec, x_spec, c_spec], compiler_params=params, name="first",
    )(pdfs, relax, fluid)
    *halo, left_goal, right_goal = exchange(ys, xs, cs, note)
    plan, table = tables(targets, left_goal, right_goal)
    post, mask, ys, xs, cs = pl.pallas_call(
        functools.partial(middle_kernel, edge), grid=(blocks,),
        out_shape=[big, jax.ShapeDtypeStruct(fluid.shape, jnp.int32)] + halo_out,
        in_specs=[full, below, above, cell, cell, cell_below, cell_above,
                  y_spec, x_all, c_spec],
        out_specs=[full, cell, y_spec, x_spec, c_spec],
        scratch_shapes=[pltpu.VMEM((q, rows, width), f32)], compiler_params=params, name="middle",
    )(post, post, post, relax, fluid, fluid, fluid, *halo)
    halo = exchange(ys, xs, cs)
    def moved(spec, shift):
        shape = spec.block_shape
        if len(shape) == 3:
            return pl.BlockSpec(shape, lambda g, plan: (plan[0, g], 0, 0))
        lead = 1 if shift == 1 else 0
        return pl.BlockSpec(
            shape, lambda g, plan: (lead, jnp.minimum(jnp.maximum(plan[0, g] + shift, 0), blocks - 1), 0, 0))

    def whole(shape):
        return pl.BlockSpec(shape, lambda g, plan: (0,) * len(shape))

    def out(row):
        return pl.BlockSpec((q, 1, rows, width), lambda g, plan: (0, plan[row, g], 0, 0))

    sent = jax.ShapeDtypeStruct((q, blocks // 2, rows, width), f32)
    right, left, kept = pl.pallas_call(
        functools.partial(last_kernel, edge), out_shape=[sent, sent, big],
        grid_spec=pltpu.PrefetchScalarGridSpec(
            num_scalar_prefetch=1, grid=(blocks,),
            in_specs=[moved(cell, 0), moved(full, 0), moved(below, -1), moved(above, 1),
                      whole(y_shape), whole(x_shape), whole(c_shape)],
            out_specs=[out(2), out(3), out(4)],
            scratch_shapes=[pltpu.VMEM((q, 1, rows, width), f32)]),
        compiler_params=params, name="last",
    )(plan, mask, post, post, post, *halo)
    from_left, from_right = migrate(right, left)
    return place(kept, from_left, from_right, table)


def solution(mesh):
    placed = (
        P(None, None, "bxy", "bz"),
        P(None, "bxy", "bz"),
        P(None, "bxy", "bz"),
        P("bz", "bxy", None),
    )
    return jax.shard_map(
        on_device, mesh=mesh, in_specs=placed, out_specs=P(None, None, "bxy", "bz"), check_vma=False
    )
```

```python
import functools
import math

import jax
import jax.numpy as jnp
from jax import lax
from jax.experimental import pallas as pl
from jax.experimental.pallas import tpu as pltpu
from jax.sharding import PartitionSpec as P

MESH = pl.DeviceIdType.MESH
VELOCITIES = (
    (0, 0, 0), (1, 0, 0), (-1, 0, 0), (0, 1, 0), (0, -1, 0), (0, 0, 1), (0, 0, -1),
    (1, 1, 0), (-1, -1, 0), (1, -1, 0), (-1, 1, 0), (1, 0, 1), (-1, 0, -1),
    (1, 0, -1), (-1, 0, 1), (0, 1, 1), (0, -1, -1), (0, 1, -1), (0, -1, 1),
)
OPPOSITE = (0, 2, 1, 4, 3, 6, 5, 8, 7, 10, 9, 12, 11, 14, 13, 16, 15, 18, 17)
Q = 19
ORDER = (5, 11, 14, 15, 18, 6, 12, 13, 16, 17, 0, 1, 2, 3, 4, 7, 8, 9, 10)
AT = tuple(ORDER.index(i) for i in range(Q))
NATURAL = tuple(range(Q))
Y_SENT = tuple(tuple(i for i in range(Q) if VELOCITIES[i][1] == c) for c in (1, -1))
X_SENT = tuple(tuple(i for i in range(Q) if VELOCITIES[i][0] == c) for c in (1, -1))
CORNERS = (7, 8, 9, 10)
SIDE = {1: 0, -1: 1}
VMEM_LIMIT = 60 * 1024 * 1024


def collide(f, rate):
    pair = {i: (f[i] + f[i + 1], f[i] - f[i + 1]) for i in range(1, Q, 2)}
    density = f[0]
    for i in range(1, Q, 2):
        density = density + pair[i][0]
    scale = 3.0 / density
    flow = []
    for axis in range(3):
        total = None
        for i in range(1, Q, 2):
            c = VELOCITIES[i][axis]
            if c:
                d = pair[i][1]
                total = d if total is None else (total + d if c == 1 else total - d)
        flow.append(total * scale)
    base = 1.0 - (flow[0] * flow[0] + flow[1] * flow[1] + flow[2] * flow[2]) * (1.0 / 6.0)
    keep = 1.0 - rate
    drive = rate * density
    post = [None] * Q
    post[0] = keep * f[0] + (drive * (1.0 / 3.0)) * base
    near, far = drive * (1.0 / 18.0), drive * (1.0 / 36.0)
    for i in range(1, Q, 2):
        along = None
        for axis in range(3):
            c = VELOCITIES[i][axis]
            if c:
                along = flow[axis] if along is None else (along + flow[axis] if c == 1 else along - flow[axis])
        even = base + 0.5 * (along * along)
        weight = near if i < 7 else far
        post[i] = keep * f[i] + weight * (even + along)
        post[i + 1] = keep * f[i + 1] + weight * (even - along)
    return post


def collide_block(read, relax_ref, fluid_ref, post_ref):
    rows, width = relax_ref.shape[1:]
    tiles = width // 128

    def body(step, carry):
        r = pl.multiple_of((step // tiles) * 8, 8)
        c = pl.multiple_of((step % tiles) * 128, 128)
        at = (pl.ds(r, 8), pl.ds(c, 128))
        rate = jnp.where(fluid_ref[(0,) + at] > 0, relax_ref[(0,) + at], 0.0)
        post = collide([read(i, at) for i in range(Q)], rate)
        for i in range(Q):
            post_ref[(AT[i], 0) + at] = post[i]
        return carry

    lax.fori_loop(0, (rows // 8) * tiles, body, 0, unroll=4)


def emit_halo(slot, last, edge, post_ref, fluid_ref, ys_ref, xs_ref, cs_ref):
    rows, width = fluid_ref.shape[1:]
    lane = lax.broadcasted_iota(jnp.int32, (rows, 128), 1)
    mine = lane // edge == slot
    for side, first in ((0, width - 128), (1, 0)):
        turn = slot * edge + (edge if side == 0 else 0)
        turn = lax.rem(turn, 128)
        for n in range(6):
            if n < 5:
                tile = post_ref[AT[Y_SENT[side][n]], 0, :, first:first + 128]
            else:
                tile = fluid_ref[0, :, first:first + 128].astype(jnp.float32)
            ys_ref[side, n] = jnp.where(mine, pltpu.roll(tile, turn, 1), ys_ref[side, n])
    for side, row in ((0, rows - 1), (1, 0)):
        for n in range(5):
            xs_ref[side, 0, n:n + 1, :] = post_ref[AT[X_SENT[side][n]], 0, row:row + 1, :]
        xs_ref[side, 0, 5:6, :] = fluid_ref[0, row:row + 1, :].astype(jnp.float32)
        xs_ref[side, 0, 6:8, :] = jnp.zeros((2, width), jnp.float32)

    @pl.when(last)
    def _():
        for k, i in enumerate(CORNERS):
            cx, cy, _z = VELOCITIES[i]
            row = rows - 1 if cx == 1 else 0
            ys = SIDE[cy]
            cs_ref[k, 0:1, :] = ys_ref[ys, Y_SENT[ys].index(i), row:row + 1, :]
            cs_ref[k, 1:2, :] = ys_ref[ys, 5, row:row + 1, :]
            cs_ref[k, 2:8, :] = jnp.zeros((6, 128), jnp.float32)


def first_kernel(edge, pdfs_ref, relax_ref, fluid_ref, post_ref, ys_ref, xs_ref, cs_ref):
    slot = pl.program_id(0)
    collide_block(lambda i, at: pdfs_ref[(i, 0) + at], relax_ref, fluid_ref, post_ref)
    emit_halo(slot, slot == pl.num_programs(0) - 1, edge, post_ref, fluid_ref, ys_ref, xs_ref, cs_ref)


def remote(src, dst, send_sem, recv_sem, device):
    return pltpu.make_async_remote_copy(
        src_ref=src, dst_ref=dst, send_sem=send_sem, recv_sem=recv_sem, device_id=device, device_id_type=MESH)


def halo_kernel(noted, *refs):
    ys, xs, cs = refs[:3]
    yr, xr, cr = refs[3 + noted:6 + noted]
    send_sem, recv_sem = refs[-2:]
    nz, nb = lax.axis_size("bz"), lax.axis_size("bxy")
    z, b = lax.axis_index("bz"), lax.axis_index("bxy")

    def there(dz, db):
        exists = None
        for at, step, count in ((z, dz, nz), (b, db, nb)):
            if step:
                inside = at < count - 1 if step == 1 else at > 0
                exists = inside if exists is None else exists & inside
        return exists

    routes = [(ys.at[0], yr.at[0], 1, 0), (ys.at[1], yr.at[1], -1, 0),
              (xs.at[0], xr.at[0], 0, 1), (xs.at[1], xr.at[1], 0, -1)]
    for k, i in enumerate(CORNERS):
        routes.append((cs.at[k], cr.at[k], VELOCITIES[i][1], VELOCITIES[i][0]))
    peers = [route[2:] for route in routes]
    if noted:
        note, from_left, from_right = refs[3], refs[7], refs[8]
        routes += [(note, from_left, 0, 1), (note, from_right, 0, -1)]
    barrier = pltpu.get_barrier_semaphore()
    count = 0
    for dz, db in peers:
        count = count + there(dz, db).astype(jnp.int32)

        @pl.when(there(dz, db))
        def _():
            pl.semaphore_signal(barrier, inc=1, device_id=(z + dz, b + db), device_id_type=MESH)

    pl.semaphore_wait(barrier, count)
    for n, (src, dst, dz, db) in enumerate(routes):
        @pl.when(there(dz, db))
        def _():
            remote(src, dst, send_sem.at[n], recv_sem.at[n], (z + dz, b + db)).start()

    for n, (src, dst, dz, db) in enumerate(routes):
        @pl.when(there(dz, db))
        def _():
            remote(src, dst, send_sem.at[n], recv_sem.at[n], (z + dz, b + db)).wait_send()

        @pl.when(there(-dz, -db))
        def _():
            remote(src, dst, send_sem.at[n], recv_sem.at[n], (z - dz, b - db)).wait_recv()


def exchange(ys, xs, cs, note=None):
    hbm = pl.BlockSpec(memory_space=pl.ANY)
    noted = note is not None
    sent = [ys, xs, cs] + ([note] if noted else [])
    got = sent + ([note] if noted else [])
    count = 8 + 2 * noted
    return pl.pallas_call(
        functools.partial(halo_kernel, int(noted)),
        out_shape=[jax.ShapeDtypeStruct(a.shape, a.dtype) for a in got],
        in_specs=[hbm] * len(sent),
        out_specs=[hbm] * len(got),
        scratch_shapes=[pltpu.SemaphoreType.DMA((count,)), pltpu.SemaphoreType.DMA((count,))],
        compiler_params=pltpu.CompilerParams(collective_id=0 if noted else 2, has_side_effects=True,
                                             vmem_limit_bytes=VMEM_LIMIT),
        name="halo_noted" if noted else "halo",
    )(*sent)


def lane_shift(velocity, slot, edge, here, below, above, beside):
    _cx, cy, cz = velocity
    width = here.shape[1]
    step = cy * edge + cz
    moved = here if step == 0 else pltpu.roll(here, step % width, 1)
    if cz:
        depth = lax.broadcasted_iota(jnp.int32, here.shape, 1) % edge
        other, face = (below, 0) if cz == 1 else (above, edge - 1)
        carry = step - cz * edge
        wrapped = other if carry == 0 else pltpu.roll(other, carry % width, 1)
        moved = jnp.where(depth == face, wrapped, moved)
    if cy:
        lane = lax.broadcasted_iota(jnp.int32, (here.shape[0], 128), 1)
        offset = 128 if cy == 1 else 256 - edge
        outside = pltpu.roll(beside, lax.rem(offset + cz + 128 - slot * edge, 128), 1)
        if cy == 1:
            moved = jnp.concatenate([jnp.where(lane < edge, outside, moved[:, :128]), moved[:, 128:]], axis=1)
        else:
            moved = jnp.concatenate(
                [moved[:, :-128], jnp.where(lane >= 128 - edge, outside, moved[:, -128:])], axis=1)
    return moved


def arrive(i, slot, edge, slots, here, below, above, yr_ref, xr_ref, cr_ref, fluid):
    velocity = cx, cy, cz = VELOCITIES[i]
    beside = None
    if cy:
        side = SIDE[cy]
        beside = yr_ref[side, 5 if fluid else Y_SENT[side].index(i)]
    moved = lane_shift(velocity, slot, edge, here, below, above, beside)
    if cx:
        side = SIDE[cx]
        row = 5 if fluid else X_SENT[side].index(i)
        rows = moved.shape[0]

        def plane(s):
            return jnp.broadcast_to(xr_ref[side, s, row:row + 1, :], (8, moved.shape[1]))

        corner = None
        if cy:
            k = CORNERS.index(i)
            n = 1 if fluid else 0
            corner = jnp.broadcast_to(cr_ref[k, n:n + 1, :], (8, 128))
        entering = lane_shift(
            velocity, slot, edge, plane(slot), plane(jnp.maximum(slot - 1, 0)) if cz == 1 else None,
            plane(jnp.minimum(slot + 1, slots - 1)) if cz == -1 else None, corner)
        index = lax.broadcasted_iota(jnp.int32, (8, moved.shape[1]), 0)
        moved = pltpu.roll(moved, cx % rows, 0)
        if cx == 1:
            moved = jnp.concatenate([jnp.where(index == 0, entering, moved[:8]), moved[8:]], axis=0)
        else:
            moved = jnp.concatenate([moved[:-8], jnp.where(index == 7, entering, moved[-8:])], axis=0)
    return moved


def stream_block(slot, edge, slots, mask_ref, post_ref, below_ref, above_ref, yr_ref, xr_ref, cr_ref, write):
    for i in range(Q):
        cz = VELOCITIES[i][2]
        own = post_ref[AT[i], 0]
        if i == 0:
            write(0, own)
            continue
        value = arrive(
            i, slot, edge, slots, own, below_ref[AT[i], 0] if cz == 1 else None,
            above_ref[AT[i] - 5, 0] if cz == -1 else None, yr_ref, xr_ref, cr_ref, False)
        mask = mask_ref[0]
        stay = jnp.where(mask > 0, post_ref[AT[OPPOSITE[i]], 0], own)
        write(i, jnp.where((mask & (1 << i)) != 0, value, stay))


def middle_kernel(edge, post_ref, below_ref, above_ref, relax_ref, fluid_ref, fbelow_ref, fabove_ref,
                  yr_ref, xr_ref, cr_ref, out_ref, mask_ref, ys_ref, xs_ref, cs_ref, next_ref):
    slot, slots = pl.program_id(0), pl.num_programs(0)
    rows, width = fluid_ref.shape[1:]
    row = lax.broadcasted_iota(jnp.int32, (rows, width), 0)
    lane = lax.broadcasted_iota(jnp.int32, (rows, width), 1)
    depth = lane % edge
    z, b = lax.axis_index("bz"), lax.axis_index("bxy")
    at_end = (b == 0, b == lax.axis_size("bxy") - 1, z == 0, z == lax.axis_size("bz") - 1)
    fluid = fluid_ref[0].astype(jnp.float32)
    bits = jnp.ones((rows, width), jnp.int32)
    for i in range(1, Q):
        cx, cy, cz = VELOCITIES[i]
        source = arrive(i, slot, edge, slots, fluid, fbelow_ref[0].astype(jnp.float32) if cz == 1 else None,
                        fabove_ref[0].astype(jnp.float32) if cz == -1 else None, yr_ref, xr_ref, cr_ref, True)
        bit = jnp.where(source > 0.5, 1 << i, 0)
        if cx:
            edge_row = 0 if cx == 1 else rows - 1
            bit = jnp.where((row == edge_row) & at_end[0 if cx == 1 else 1], 0, bit)
        if cy:
            outer = lane < edge if cy == 1 else lane >= width - edge
            bit = jnp.where(outer & at_end[2 if cy == 1 else 3], 0, bit)
        if cz:
            final = 0 if cz == 1 else slots - 1
            face = 0 if cz == 1 else edge - 1
            bit = jnp.where((depth == face) & (slot == final), 0, bit)
        bits = bits | bit
    mask_ref[0] = jnp.where(fluid_ref[0] > 0, bits, 0)

    def write(i, value):
        next_ref[i] = value

    stream_block(slot, edge, slots, mask_ref, post_ref, below_ref, above_ref, yr_ref, xr_ref, cr_ref, write)
    collide_block(lambda i, at: next_ref[(i,) + at], relax_ref, fluid_ref, out_ref)
    emit_halo(slot, slot == slots - 1, edge, out_ref, fluid_ref, ys_ref, xs_ref, cs_ref)


def last_kernel(edge, plan_ref, mask_ref, post_ref, below_ref, above_ref, yr_ref, xr_ref, cr_ref,
                right_ref, left_ref, kept_ref, next_ref):
    def write(i, value):
        next_ref[i, 0] = value

    g = pl.program_id(0)
    stream_block(plan_ref[0, g], edge, pl.num_programs(0), mask_ref, post_ref, below_ref, above_ref,
                 yr_ref, xr_ref, cr_ref, write)
    for kind, out_ref in enumerate((right_ref, left_ref, kept_ref)):
        @pl.when(plan_ref[1, g] == kind)
        def _():
            def copy(i, carry):
                out_ref[i] = next_ref[i]
                return carry

            lax.fori_loop(0, Q, copy, 0)


def migrate_kernel(right, left, from_left, from_right, passing, send_sem, recv_sem):
    nb = lax.axis_size("bxy")
    z, b = lax.axis_index("bz"), lax.axis_index("bxy")
    half = (Q + 1) // 2
    cuts = (0, half // 2, half, half + (Q - half + 1) // 2, Q)
    chunks = [(n, slice(cuts[n], cuts[n + 1]), n < 2) for n in range(4)]
    across = math.isqrt(nb // 2)
    row = 2 * across
    bends = across == 2 and nb == 2 * row
    cut = row - 1 if bends else nb
    low, high = cut + 1 - row, cut + row
    no = b < 0
    goes_right, goes_left = (b < nb - 1) & (b != cut), (b > 0) & (b != cut + 1)
    at_cut, past_cut, is_low, is_high = (
        (b == cut, b == cut + 1, b == low, b == high) if bends else (no, no, no, no))
    meets = [(goes_right, b + 1), (goes_left, b - 1)]
    if bends:
        for who in (at_cut, past_cut):
            meets += [(who, low), (who, high)]
        for who in (is_low, is_high):
            meets += [(who, cut), (who, cut + 1)]
    barrier = pltpu.get_barrier_semaphore()
    count = 0
    for who, peer in meets:
        count = count + who.astype(jnp.int32)

        @pl.when(who)
        def _():
            pl.semaphore_signal(barrier, inc=1, device_id=(z, peer), device_id_type=MESH)

    pl.semaphore_wait(barrier, count)

    def copy(src, dst, c, part, sent, got, peer):
        return remote(src.at[part], dst.at[part], send_sem.at[sent, c], recv_sem.at[got, c], (z, peer))

    for c, part, first in chunks:
        @pl.when(goes_right)
        def _():
            copy(right, from_left, c, part, 0, 0, b + 1).start()

        @pl.when(goes_left)
        def _():
            copy(left, from_right, c, part, 1, 1, b - 1).start()

        if bends:
            @pl.when(at_cut)
            def _():
                copy(right, passing, c, part, 0, 2, low if first else high).start()

            @pl.when(past_cut)
            def _():
                copy(left, passing, c, part, 1, 2, high if first else low).start()

    if bends:
        for who, ahead in ((is_low, True), (is_high, False)):
            @pl.when(who)
            def _():
                for n in (0, 2, 1, 3):
                    c, part, first = chunks[n]
                    copy(right, passing, c, part, 2, 2, cut).wait_recv()
                    if first == ahead:
                        copy(passing, from_left, c, part, 2, 0, cut + 1).start()
                    else:
                        copy(passing, from_right, c, part, 2, 1, cut).start()
                for c, part, first in chunks:
                    copy(passing, from_left, c, part, 2, 0, cut).wait_send()

    for c, part, first in chunks:
        @pl.when(b < nb - 1)
        def _():
            copy(right, from_left, c, part, 0, 0, b + 1).wait_send()
            copy(left, from_right, c, part, 1, 1, b + 1).wait_recv()

        @pl.when(b > 0)
        def _():
            copy(left, from_right, c, part, 1, 1, b - 1).wait_send()
            copy(right, from_left, c, part, 0, 0, b - 1).wait_recv()


def migrate(right, left):
    hbm = pl.BlockSpec(memory_space=pl.ANY)
    shape = jax.ShapeDtypeStruct(right.shape, right.dtype)
    from_left, from_right, _passing = pl.pallas_call(
        migrate_kernel, out_shape=[shape] * 3, in_specs=[hbm] * 2, out_specs=[hbm] * 3,
        scratch_shapes=[pltpu.SemaphoreType.DMA((3, 4)), pltpu.SemaphoreType.DMA((3, 4))],
        compiler_params=pltpu.CompilerParams(collective_id=1, has_side_effects=True, vmem_limit_bytes=VMEM_LIMIT),
        name="migrate",
    )(right, left)
    return from_left, from_right


def place_kernel(table_ref, final_ref, left_ref, right_ref, out_ref):
    kind = table_ref[3, pl.program_id(0)]

    @pl.when(kind == 0)
    def _():
        out_ref[...] = final_ref[...]

    @pl.when(kind == 1)
    def _():
        out_ref[...] = left_ref[...]

    @pl.when(kind == 2)
    def _():
        out_ref[...] = right_ref[...]


def place(final, left, right, table):
    q, blocks, rows, width = final.shape
    parts = 1
    block = (q, 1, rows // parts, width)

    def taken(kind):
        return pl.BlockSpec(
            block, lambda k, h, table: (0, table[kind, k], jnp.where(table[3, k] == kind, h, parts - 1), 0))

    return pl.pallas_call(
        place_kernel,
        out_shape=jax.ShapeDtypeStruct(final.shape, final.dtype),
        grid_spec=pltpu.PrefetchScalarGridSpec(
            num_scalar_prefetch=1, grid=(blocks, parts),
            in_specs=[taken(0), taken(1), taken(2)],
            out_specs=pl.BlockSpec(block, lambda k, h, table: (0, k, h, 0))),
        compiler_params=pltpu.CompilerParams(vmem_limit_bytes=VMEM_LIMIT),
        name="place",
    )(table, final, left, right)


def tables_kernel(goal_ref, left_ref, right_ref, plan_ref, table_ref):
    here, owners = lax.axis_index("bxy"), lax.axis_size("bxy")
    blocks = goal_ref.shape[2]
    base = here * blocks

    def total(terms):
        return sum(t.astype(jnp.int32) for t in terms)

    goal = [goal_ref[0, 0, j] for j in range(blocks)]
    way = [jnp.where(g >= base + blocks, 0, jnp.where(g < base, 1, 2)) for g in goal]
    key = [way[j] * blocks + j for j in range(blocks)]
    at = [total(key[k] < key[j] for k in range(blocks)) for j in range(blocks)]
    rights, lefts = total(w == 0 for w in way), total(w == 1 for w in way)

    def in_order(values, position):
        return sum(jnp.where(at[j] == position, values[j], 0) for j in range(blocks))

    for g in range(blocks):
        plan_ref[0, g] = in_order(list(range(blocks)), g)
        plan_ref[1, g] = in_order(way, g)
        plan_ref[2, g] = jnp.minimum(g, jnp.maximum(rights - 1, 0))
        plan_ref[3, g] = jnp.maximum(jnp.minimum(g - rights, lefts - 1), 0)
        first = jnp.minimum(jnp.maximum(g, rights + lefts), blocks - 1)
        plan_ref[4, g] = in_order([lax.rem(v, blocks) for v in goal], first)

    kind = [jnp.int32(0)] * blocks
    index = [jnp.int32(k) for k in range(blocks)]
    for source, ref, valid in ((1, left_ref, here > 0), (2, right_ref, here < owners - 1)):
        rank = jnp.int32(0)
        for j in range(blocks):
            value = ref[j, 0]
            for k in range(blocks):
                hit = valid & (value == base + k)
                kind[k] = jnp.where(hit, source, kind[k])
                index[k] = jnp.where(hit, rank, index[k])
            rank = rank + (valid & (value >= base) & (value < base + blocks)).astype(jnp.int32)
    for source in range(3):
        held = jnp.int32(0)
        for k in range(blocks):
            held = jnp.where(kind[k] == source, index[k], held)
            table_ref[source, k] = held
    for k in range(blocks):
        table_ref[3, k] = kind[k]


def tables(targets, left_goal, right_goal):
    blocks = targets.shape[2]
    smem = pl.BlockSpec(memory_space=pltpu.SMEM)
    return pl.pallas_call(
        tables_kernel,
        out_shape=[jax.ShapeDtypeStruct((5, blocks), jnp.int32), jax.ShapeDtypeStruct((4, blocks), jnp.int32)],
        in_specs=[smem] * 3, out_specs=[smem] * 2, name="tables",
    )(targets, left_goal, right_goal)


def on_device(pdfs, relax, fluid, targets):
    q, blocks, rows, width = pdfs.shape
    edge = rows
    f32 = jnp.float32
    note = jnp.broadcast_to(targets.reshape((blocks, 1)), (blocks, 128))
    full = pl.BlockSpec((q, 1, rows, width), lambda s: (0, s, 0, 0))
    cell = pl.BlockSpec((1, rows, width), lambda s: (s, 0, 0))
    cell_below = pl.BlockSpec((1, rows, width), lambda s: (jnp.maximum(s - 1, 0), 0, 0))
    cell_above = pl.BlockSpec((1, rows, width), lambda s: (jnp.minimum(s + 1, blocks - 1), 0, 0))
    below = pl.BlockSpec((5, 1, rows, width), lambda s: (0, jnp.maximum(s - 1, 0), 0, 0))
    above = pl.BlockSpec((5, 1, rows, width), lambda s: (1, jnp.minimum(s + 1, blocks - 1), 0, 0))
    y_shape, x_shape, c_shape = (2, 6, rows, 128), (2, blocks, 8, width), (4, 8, 128)
    y_spec = pl.BlockSpec(y_shape, lambda s: (0, 0, 0, 0))
    x_all = pl.BlockSpec(x_shape, lambda s: (0, 0, 0, 0))
    x_spec = pl.BlockSpec((2, 1, 8, width), lambda s: (0, s, 0, 0))
    c_spec = pl.BlockSpec(c_shape, lambda s: (0, 0, 0))
    halo_out = [jax.ShapeDtypeStruct(s, f32) for s in (y_shape, x_shape, c_shape)]
    big = jax.ShapeDtypeStruct(pdfs.shape, f32)
    params = pltpu.CompilerParams(vmem_limit_bytes=VMEM_LIMIT)

    post, ys, xs, cs = pl.pallas_call(
        functools.partial(first_kernel, edge), grid=(blocks,),
        out_shape=[big] + halo_out, in_specs=[full, cell, cell],
        out_specs=[full, y_spec, x_spec, c_spec], compiler_params=params, name="first",
    )(pdfs, relax, fluid)
    *halo, left_goal, right_goal = exchange(ys, xs, cs, note)
    plan, table = tables(targets, left_goal, right_goal)
    post, mask, ys, xs, cs = pl.pallas_call(
        functools.partial(middle_kernel, edge), grid=(blocks,),
        out_shape=[big, jax.ShapeDtypeStruct(fluid.shape, jnp.int32)] + halo_out,
        in_specs=[full, below, above, cell, cell, cell_below, cell_above,
                  y_spec, x_all, c_spec],
        out_specs=[full, cell, y_spec, x_spec, c_spec],
        scratch_shapes=[pltpu.VMEM((q, rows, width), f32)], compiler_params=params, name="middle",
    )(post, post, post, relax, fluid, fluid, fluid, *halo)
    halo = exchange(ys, xs, cs)
    def moved(spec, shift):
        shape = spec.block_shape
        if len(shape) == 3:
            return pl.BlockSpec(shape, lambda g, plan: (plan[0, g], 0, 0))
        lead = 1 if shift == 1 else 0
        return pl.BlockSpec(
            shape, lambda g, plan: (lead, jnp.minimum(jnp.maximum(plan[0, g] + shift, 0), blocks - 1), 0, 0))

    def whole(shape):
        return pl.BlockSpec(shape, lambda g, plan: (0,) * len(shape))

    def out(row):
        return pl.BlockSpec((q, 1, rows, width), lambda g, plan: (0, plan[row, g], 0, 0))

    sent = jax.ShapeDtypeStruct((q, blocks // 2, rows, width), f32)
    right, left, kept = pl.pallas_call(
        functools.partial(last_kernel, edge), out_shape=[sent, sent, big],
        grid_spec=pltpu.PrefetchScalarGridSpec(
            num_scalar_prefetch=1, grid=(blocks,),
            in_specs=[moved(cell, 0), moved(full, 0), moved(below, -1), moved(above, 1),
                      whole(y_shape), whole(x_shape), whole(c_shape)],
            out_specs=[out(2), out(3), out(4)],
            scratch_shapes=[pltpu.VMEM((q, 1, rows, width), f32)]),
        compiler_params=params, name="last",
    )(plan, mask, post, post, post, *halo)
    from_left, from_right = migrate(right, left)
    return place(kept, from_left, from_right, table)


def solution(mesh):
    placed = (
        P(None, None, "bxy", "bz"),
        P(None, "bxy", "bz"),
        P(None, "bxy", "bz"),
        P("bz", "bxy", None),
    )
    return jax.shard_map(
        on_device, mesh=mesh, in_specs=placed, out_specs=P(None, None, "bxy", "bz"), check_vma=False
    )
```
